32 devices in a mesh: tm: 2 (over core), tile: 16 (over z, y, x).
Axes of the slice: x: 2, y: 2, z: 4, core: 2. Of those that a mesh axis runs over, the one named last changes fastest.
Arguments:
- frames: bfloat16 [8, 16, 64, 32, 128], P('tm', 'tile'), may hold values from -6 to 6
- w_in: bfloat16 [3, 3, 128, 128], replicated, may hold values from -0.1875 to 0.1875
- w_out: bfloat16 [3, 3, 128, 128], replicated, may hold values from -0.1875 to 0.1875
- decay: float32 [8, 128], P('tm'), may hold values from 0 to 1
- skip: float32 [128], replicated, may hold values from 0.5 to 1.5
Outputs:
- mixed: bfloat16 [8, 16, 64, 32, 128], P('tm', 'tile')
The draws below stay inside these ranges and needn't reach their ends.
All inputs are finite; a program needn't handle non-finite values.
Results may differ from the reference program's by a relative error of at most 0.006.
Values may be sent and summed in bfloat16 or wider, within the bound.
No kernel may reach another device: no remote copies, remote signals or barrier semaphores. Data moves between devices by JAX's collectives and lax.ppermute only.
A program may use at most 64 MiB of HBM per device.

```python
import jax
import jax.numpy as jnp
from jax import lax

C = 128
STATE_CHANNELS = 128
TH = 64
TW = 32
TROWS = 4
WINDOW_FRAMES = 8
TILES = 16
TCOLS = 4


def draw_decay(key, part):
    sampler_keys = jax.random.split(key, 6)
    fast_rate = 0.05 ** (1.0 / jax.random.uniform(sampler_keys[0], (STATE_CHANNELS,), jnp.float32, 30.0, 50.0))
    slow_rate = 0.3 ** (1.0 / (WINDOW_FRAMES * jax.random.uniform(sampler_keys[1], (STATE_CHANNELS,), jnp.float32, 0.7, 1.0)))
    fast_mask = jax.random.randint(sampler_keys[2], (STATE_CHANNELS,), 0, 2) == 1
    resting_rate = jnp.where(fast_mask, fast_rate, slow_rate)
    noise_multiplier = jax.random.uniform(sampler_keys[3], (WINDOW_FRAMES, STATE_CHANNELS), jnp.float32, 0.97, 1.0)
    spike_events = jax.random.randint(sampler_keys[4], (WINDOW_FRAMES, 1), 0, 8) == 0
    spike_keep_mask = jax.random.uniform(sampler_keys[5], (WINDOW_FRAMES, STATE_CHANNELS), jnp.float32, 0.5, 0.8)
    return (resting_rate[None, :] * noise_multiplier * jnp.where(spike_events, spike_keep_mask, 1.0)).astype(jnp.float32)


def shard_levels(stream_key, extent, shards, low, largest):
    def one(axis_at, blocks):
        heights = jax.random.uniform(jax.random.fold_in(jax.random.fold_in(stream_key, 6), axis_at), (blocks,), jnp.float32, low / len(shards), largest / len(shards))
        return jnp.repeat(jnp.exp(heights), extent[axis_at] // blocks).reshape((-1,) + (1,) * (len(extent) - axis_at - 1))

    factor_of = one(*shards[0])
    for cut in shards[1:]:
        factor_of = factor_of * one(*cut)
    return factor_of


def gaussian(stream_key, extent, width, most, cuts=(), dtype=jnp.bfloat16):
    drawn = width * jax.random.normal(stream_key, extent, jnp.float32)
    if cuts:
        drawn = drawn * shard_levels(stream_key, extent, cuts, -0.22, 0.18)
    return jnp.clip(drawn, -most, most).astype(dtype)


def setup_inputs(seed: int = 0) -> dict:
    arg_keys = jax.random.split(jax.random.key(seed), 6)
    frames = gaussian(arg_keys[0], (WINDOW_FRAMES, TILES, TH, TW, C), 1.0, 6.0, ((0, 2), (1, 16)))
    w_in = gaussian(arg_keys[1], (3, 3, C, STATE_CHANNELS), (9 * C) ** -0.5, 0.1875)
    w_out = gaussian(arg_keys[2], (3, 3, STATE_CHANNELS, C), (9 * STATE_CHANNELS) ** -0.5, 0.1875)
    decay = draw_decay(jax.random.fold_in(arg_keys[5], 71), 0)
    skip = jnp.clip(jax.random.uniform(arg_keys[4], (C,), jnp.float32, 0.5, 1.5), 0.5, 1.5)
    return {"frames": frames, "w_in": w_in, "w_out": w_out, "decay": decay, "skip": skip}


def build_sequence(tiled):
    count = tiled.shape[0]
    ordered = jnp.roll(tiled, -1, axis=1)
    grid = ordered.reshape(count, TROWS, TCOLS, TH, TW, tiled.shape[-1])
    return grid.transpose(0, 1, 3, 2, 4, 5).reshape(count, TROWS * TH, TCOLS * TW, tiled.shape[-1])


def disassemble(image):
    count = image.shape[0]
    grid = image.reshape(count, TROWS, TH, TCOLS, TW, image.shape[-1])
    ordered = grid.transpose(0, 1, 3, 2, 4, 5).reshape(count, TROWS * TCOLS, TH, TW, image.shape[-1])
    return jnp.roll(ordered, 1, axis=1)


def convolve(picture, weight):
    result = lax.conv_general_dilated(picture[None].astype(jnp.float32), weight.astype(jnp.float32), (1, 1), "SAME", dimension_numbers=("NHWC", "HWIO", "NHWC"), precision=lax.Precision.HIGHEST)
    return result[0]


def reference(frames, w_in, w_out, decay, skip):
    image = build_sequence(frames)

    def advance(state, inputs):
        picture, keep_fraction = inputs
        drive = convolve(picture, w_in)
        state = keep_fraction * state + drive
        state_bf = lax.optimization_barrier(state.astype(jnp.bfloat16))
        mixed = convolve(state_bf, w_out) + skip * picture.astype(jnp.float32)
        return state, mixed.astype(jnp.bfloat16)

    start = jnp.zeros((TROWS * TH, TCOLS * TW, STATE_CHANNELS), jnp.float32)
    final_state, outputs = lax.scan(advance, start, (image, decay))
    return disassemble(outputs)
```

```python
import functools

import jax
import jax.numpy as jnp
from jax import lax
from jax.experimental import pallas as pl
from jax.experimental.pallas import tpu as pltpu
from jax.sharding import PartitionSpec as P

TROWS = 4
BF = jnp.bfloat16
F32 = jnp.float32
LIMIT = 24 << 20
BLOCK = 16
VM = pl.BlockSpec(memory_space=pltpu.VMEM)


def shifted(value, axis, by):
    size = lax.axis_size(axis)
    return lax.ppermute(value, axis, [(i, (i + by) % size) for i in range(size)])


def place():
    count = lax.axis_size("tile")
    tcols = count // TROWS
    number = lax.rem(lax.axis_index("tile") + count - 1, count)
    return lax.rem(number, tcols), lax.div(number, tcols), tcols


def dot(a, b):
    return jnp.dot(a, b, preferred_element_type=F32)


def spread(w_ref, wide):
    c, n = w_ref.shape[2:]
    zero = jnp.zeros((c, n), BF)
    for tap in range(3):
        for row in range(4):
            for out in range(2):
                at = tap * 2 * n + out * n
                k = row - out
                wide[row * c : (row + 1) * c, at : at + n] = w_ref[k, tap] if 0 <= k <= 2 else zero


def gathered(y, pairs, cols, n2):
    y = y.reshape(pairs, cols, 3 * n2)
    left, mid, right = y[:, :, :n2], y[:, :, n2 : 2 * n2], y[:, :, 2 * n2 :]
    col = lax.broadcasted_iota(jnp.int32, mid.shape, 1)
    left = jnp.where(col > 0, pltpu.roll(left, 1, 1), 0.0)
    right = jnp.where(col < cols - 1, pltpu.roll(right, cols - 1, 1), 0.0)
    return mid + left + right


def gathered_edge(y, pairs, n2):
    y = y.reshape(pairs, 8, 3 * n2)
    left, mid, right = y[:, :, :n2], y[:, :, n2 : 2 * n2], y[:, :, 2 * n2 :]
    col = lax.broadcasted_iota(jnp.int32, mid.shape, 1)
    full = (col == 2) | (col == 5)
    left = jnp.where(full | (col == 6), pltpu.roll(left, 1, 1), 0.0)
    right = jnp.where(full | (col == 1), pltpu.roll(right, 7, 1), 0.0)
    return jnp.where(full, mid, 0.0) + left + right


def blocks(pairs):
    return [(q, min(BLOCK, pairs - q)) for q in range(1, pairs, BLOCK)]


def main_kernel(x_ref, w_ref, d_ref, s_ref, wide):
    frames, pairs, _, cols, c = x_ref.shape
    n2 = s_ref.shape[3]
    spread(w_ref, wide)

    def rows(f, p, n):
        return jnp.concatenate(
            [x_ref[f, p : p + n, r].reshape(n * cols, c) for r in range(2)], axis=-1
        )

    for q, n in [(0, 1), *blocks(pairs), (pairs, 1)]:
        state = None
        for f in range(frames):
            y = None
            if q > 0:
                y = dot(rows(f, q - 1, n), wide[: 2 * c])
            if q < pairs:
                low = dot(rows(f, q, n), wide[2 * c :])
                y = low if y is None else y + low
            y = gathered(y, n, cols, n2)
            keep = jnp.concatenate([d_ref[f : f + 1]] * 2, axis=-1).reshape(1, 1, n2)
            state = y if f == 0 else keep * state + y
            s_ref[f, q : q + n] = state


def edge_kernel(x_ref, lo_ref, hi_ref, fl_ref, fr_ref, e_ref, top_ref, bot_ref):
    frames, pairs, _, cols, c = x_ref.shape
    column, _, tcols = place()
    has_left, has_right = column > 0, column < tcols - 1
    for f in range(frames):
        for r in range(2):
            lane = pl.ds(r * c, c)
            e_ref[f, :, 0:2, lane] = hi_ref[f, :, r]
            e_ref[f, :, 2:4, lane] = jnp.where(has_right, fr_ref[f, :, r], 0).astype(BF)
            e_ref[f, :, 4:6, lane] = jnp.where(has_left, fl_ref[f, :, r], 0).astype(BF)
            e_ref[f, :, 6:8, lane] = lo_ref[f, :, r]
            top_ref[f, 0:cols, lane] = x_ref[f, 0, r]
            bot_ref[f, 0:cols, lane] = x_ref[f, pairs - 1, r]
        top_ref[f, cols:, :] = e_ref[f, 0]
        bot_ref[f, cols:, :] = e_ref[f, pairs - 1]


def ring_kernel(e_ref, up_ref, dn_ref, s_ref, w_ref, d_ref, r_ref, c_ref, m_ref, wide):
    frames, pairs, _, c2 = e_ref.shape
    n2 = r_ref.shape[3]
    cols = up_ref.shape[1] - 8
    _, row, _ = place()
    has_up, has_dn = row > 0, row < TROWS - 1
    spread(w_ref, wide)
    state = None
    rim = [None, None]
    for f in range(frames):
        keep = jnp.concatenate([d_ref[f : f + 1]] * 2, axis=-1).reshape(1, 1, n2)
        e = e_ref[f].reshape(pairs * 8, c2)
        high, low = dot(e, wide[:c2]), dot(e, wide[c2:])
        blank = jnp.zeros((8, 3 * n2), F32)
        y = jnp.concatenate([blank, high]) + jnp.concatenate([low, blank])
        y = gathered_edge(y, pairs + 1, n2)
        state = y if f == 0 else keep * state + y
        r_ref[f] = state
        for side, (ref, there) in enumerate(((up_ref, has_up), (dn_ref, has_dn))):
            v = jnp.where(there, ref[f], 0).astype(BF)
            y = dot(v, wide[c2:] if side else wide[:c2])
            mid = gathered(y[:cols], 1, cols, n2)
            end = gathered_edge(y[cols:], 1, n2)
            y = jnp.concatenate([mid, end], axis=1)
            rim[side] = y if f == 0 else keep * rim[side] + y
            c_ref[f, side : side + 1] = rim[side][:, :cols]
            at = side * pairs
            r_ref[f, at : at + 1] = r_ref[f, at : at + 1] + rim[side][:, cols:]
    last = frames - 1
    whole, ends = merged(s_ref, r_ref, c_ref, last)
    m_ref[:, :cols] = whole.astype(BF)
    m_ref[:, cols:] = ends.astype(BF)


def merged(s_ref, r_ref, c_ref, f):
    rim = c_ref[f]
    body = s_ref[f]
    n, cols, n2 = body.shape
    body = jnp.concatenate([body[:1] + rim[:1], body[1 : n - 1], body[n - 1 :] + rim[1:]])
    ends = r_ref[f]
    col = lax.broadcasted_iota(jnp.int32, ends.shape, 1)
    first = body[:, :8] + jnp.where(col == 0, pltpu.roll(ends, 2, 1), 0.0)
    final = body[:, cols - 8 :] + jnp.where(col == 7, pltpu.roll(ends, 6, 1), 0.0)
    return jnp.concatenate([first, body[:, 8 : cols - 8], final], axis=1), ends


def read_kernel(
    s_ref, r_ref, c_ref, m_ref, w_ref, d_ref, skip_ref, x_ref, o_ref, wide, held, ends_held, out, sems
):
    frames, pairs, _, cols, c = x_ref.shape
    n2 = s_ref.shape[3]
    spread(w_ref, wide)
    column, row, tcols = place()
    later = (lax.axis_index("tm") > 0).astype(F32)
    has_up, has_dn = row > 0, row < TROWS - 1
    has_left, has_right = column > 0, column < tcols - 1
    gain = jnp.concatenate([skip_ref[...]] * 2, axis=-1)
    factor = jnp.full((1, n2), 1.0, F32) * later
    lane = lax.broadcasted_iota(jnp.int32, (1, 1, n2), 2)
    copies = []
    for f in range(frames):
        factor = factor * jnp.concatenate([d_ref[f : f + 1]] * 2, axis=-1)
        body, ends = merged(s_ref, r_ref, c_ref, f)
        far = factor.reshape(1, 1, n2)
        body = body + far * m_ref[:, :cols].astype(F32)
        ends = ends + far * m_ref[:, cols:].astype(F32)
        col = lax.broadcasted_iota(jnp.int32, ends.shape, 1)
        ends = jnp.where(((col == 2) & has_right) | ((col == 5) & has_left), ends, 0.0)
        for value, ref in ((body, held), (ends, ends_held)):
            ref[...] = value.astype(BF)
            ref[0:1] = jnp.where(has_up | (lane >= n2 // 2), value[0:1], 0.0).astype(BF)
            ref[pairs : pairs + 1] = jnp.where(
                has_dn | (lane < n2 // 2), value[pairs : pairs + 1], 0.0
            ).astype(BF)
        for p in range(0, pairs, BLOCK):
            n = min(BLOCK, pairs - p)
            y = dot(held[p : p + n].reshape(n * cols, n2), wide[:n2])
            y = y + dot(held[p + 1 : p + 1 + n].reshape(n * cols, n2), wide[n2:])
            y = gathered(y, n, cols, n2)
            e = dot(ends_held[p : p + n].reshape(n * 8, n2), wide[:n2])
            e = e + dot(ends_held[p + 1 : p + 1 + n].reshape(n * 8, n2), wide[n2:])
            e = e.reshape(n, 8, 3 * n2)
            col = lax.broadcasted_iota(jnp.int32, (n, 8, n2), 1)
            first = y[:, :8] + jnp.where(col == 0, pltpu.roll(e[:, :, :n2], 3, 1), 0.0)
            final = y[:, cols - 8 :] + jnp.where(col == 7, pltpu.roll(e[:, :, 2 * n2 :], 5, 1), 0.0)
            y = jnp.concatenate([first, y[:, 8 : cols - 8], final], axis=1)
            half = n2 // 2
            for r in range(2):
                v = y[:, :, r * half : (r + 1) * half]
                v = v + gain[:, :half].reshape(1, 1, half) * x_ref[f, p : p + n, r].astype(F32)
                out[f, p : p + n, r] = v.astype(BF)
        copy = pltpu.make_async_copy(out.at[f], o_ref.at[f], sems.at[f])
        copy.start()
        copies.append(copy)
    for copy in copies:
        copy.wait()


def call(body, outs, ins, scratch=(), out_specs=None, name=None):
    return pl.pallas_call(
        body,
        out_shape=outs,
        in_specs=[VM] * len(ins),
        out_specs=out_specs if out_specs is not None else jax.tree.map(lambda _: VM, outs),
        scratch_shapes=list(scratch),
        compiler_params=pltpu.CompilerParams(vmem_limit_bytes=LIMIT),
        name=name,
    )(*ins)


def per_device(frames, w_in, w_out, decay, skip):
    shape = jax.ShapeDtypeStruct
    count, _, rows, cols, c = frames.shape
    n2 = 2 * w_in.shape[3]
    pairs = rows // 2
    tcols = lax.axis_size("tile") // TROWS
    video = frames.reshape(count, pairs, 2, cols, c)
    low, high = video[:, :, :, :2], video[:, :, :, cols - 2 :]
    from_left = shifted(high, "tile", 1)
    from_right = shifted(low, "tile", -1)
    local = call(
        main_kernel,
        shape((count, pairs + 1, cols, n2), F32),
        (video, w_in, decay),
        [pltpu.VMEM((4 * c, 3 * n2), BF)],
        name="main",
    )
    edge, top, bottom = call(
        edge_kernel,
        (
            shape((count, pairs, 8, 2 * c), BF),
            shape((count, cols + 8, 2 * c), BF),
            shape((count, cols + 8, 2 * c), BF),
        ),
        (video, low, high, from_left, from_right),
        name="edge",
    )
    above = shifted(bottom, "tile", tcols)
    below = shifted(top, "tile", -tcols)
    ends, rim, message = call(
        ring_kernel,
        (
            shape((count, pairs + 1, 8, n2), F32),
            shape((count, 2, cols, n2), F32),
            shape((pairs + 1, cols + 8, n2), BF),
        ),
        (edge, above, below, local, w_in, decay),
        [pltpu.VMEM((4 * c, 3 * n2), BF)],
        name="ring",
    )
    before = shifted(message, "tm", 1)
    mixed = call(
        read_kernel,
        shape((count, pairs, 2, cols, c), BF),
        (local, ends, rim, before, w_out, decay, skip.reshape(1, c), video),
        [
            pltpu.VMEM((2 * n2, 3 * 2 * c), BF),
            pltpu.VMEM((pairs + 1, cols, n2), BF),
            pltpu.VMEM((pairs + 1, 8, n2), BF),
            pltpu.VMEM((count, pairs, 2, cols, c), BF),
            pltpu.SemaphoreType.DMA((count,)),
        ],
        out_specs=pl.BlockSpec(memory_space=pl.ANY),
        name="read",
    )
    return mixed.reshape(count, 1, rows, cols, c)


def solution(mesh):
    return jax.shard_map(
        per_device,
        mesh=mesh,
        in_specs=(P("tm", "tile", None, None, None), P(), P(), P("tm", None), P()),
        out_specs=P("tm", "tile", None, None, None),
        check_vma=False,
    )
```

```python
import functools

import jax
import jax.numpy as jnp
from jax import lax
from jax.experimental import pallas as pl
from jax.experimental.pallas import tpu as pltpu
from jax.sharding import PartitionSpec as P

TROWS = 4
BF = jnp.bfloat16
F32 = jnp.float32
LIMIT = 24 << 20
BLOCK = 16
VM = pl.BlockSpec(memory_space=pltpu.VMEM)
ANY = pl.BlockSpec(memory_space=pl.ANY)


def swapped(value, across, first):
    count = lax.axis_size("tile")
    tcols = count // TROWS
    pairs = []
    for number in range(count):
        row, column = divmod(number, tcols)
        at, size = (column, tcols) if across else (row, TROWS)
        other = at + 1 if at >= first and (at - first) % 2 == 0 else at - 1
        if not first <= other < size:
            other = at
        there = row * tcols + other if across else other * tcols + column
        pairs.append(((number + 1) % count, (there + 1) % count))
    return lax.ppermute(value, "tile", pairs)


def place():
    count = lax.axis_size("tile")
    tcols = count // TROWS
    number = lax.rem(lax.axis_index("tile") + count - 1, count)
    return lax.rem(number, tcols), lax.div(number, tcols), tcols


def dot(a, b):
    return jnp.dot(a, b, preferred_element_type=F32)


def spread(w_ref, wide):
    c, n = w_ref.shape[2:]
    zero = jnp.zeros((c, n), BF)
    for tap in range(3):
        for row in range(4):
            for out in range(2):
                at = tap * 2 * n + out * n
                k = row - out
                wide[row * c : (row + 1) * c, at : at + n] = w_ref[k, tap] if 0 <= k <= 2 else zero


def gathered(y, pairs, cols, n2):
    y = y.reshape(pairs, cols, 3 * n2)
    left, mid, right = y[:, :, :n2], y[:, :, n2 : 2 * n2], y[:, :, 2 * n2 :]
    col = lax.broadcasted_iota(jnp.int32, mid.shape, 1)
    left = jnp.where(col > 0, pltpu.roll(left, 1, 1), 0.0)
    right = jnp.where(col < cols - 1, pltpu.roll(right, cols - 1, 1), 0.0)
    return mid + left + right


def gathered_edge(y, pairs, n2):
    y = y.reshape(pairs, 8, 3 * n2)
    left, mid, right = y[:, :, :n2], y[:, :, n2 : 2 * n2], y[:, :, 2 * n2 :]
    col = lax.broadcasted_iota(jnp.int32, mid.shape, 1)
    full = (col == 2) | (col == 5)
    left = jnp.where(full | (col == 6), pltpu.roll(left, 1, 1), 0.0)
    right = jnp.where(full | (col == 1), pltpu.roll(right, 7, 1), 0.0)
    return jnp.where(full, mid, 0.0) + left + right


def blocks(pairs):
    return [(q, min(BLOCK, pairs - q)) for q in range(1, pairs, BLOCK)]


def main_kernel(x_ref, w_ref, d_ref, s_ref, wide):
    frames, pairs, _, cols, c = x_ref.shape
    n2 = s_ref.shape[3]
    spread(w_ref, wide)

    def rows(f, p, n):
        return jnp.concatenate(
            [x_ref[f, p : p + n, r].reshape(n * cols, c) for r in range(2)], axis=-1
        )

    for q, n in [(0, 1), *blocks(pairs), (pairs, 1)]:
        state = None
        for f in range(frames):
            y = None
            if q > 0:
                y = dot(rows(f, q - 1, n), wide[: 2 * c])
            if q < pairs:
                low = dot(rows(f, q, n), wide[2 * c :])
                y = low if y is None else y + low
            y = gathered(y, n, cols, n2)
            keep = jnp.concatenate([d_ref[f : f + 1]] * 2, axis=-1).reshape(1, 1, n2)
            state = y if f == 0 else keep * state + y
            s_ref[f, q : q + n] = state


def pack_kernel(f_ref, x_ref, a_ref, b_ref, sems):
    frames, _, _, cols, _ = x_ref.shape
    column, _, _ = place()
    even = lax.rem(column, 2) == 0
    copies = [
        pltpu.make_async_copy(f_ref.at[f], x_ref.at[f], sems.at[f]) for f in range(frames)
    ]
    for copy in copies:
        copy.start()
    for f, copy in enumerate(copies):
        copy.wait()
        low, high = x_ref[f, :, :, :2], x_ref[f, :, :, cols - 2 :]
        a_ref[f] = jnp.where(even, high, low)
        b_ref[f] = jnp.where(even, low, high)


def edge_kernel(x_ref, fa_ref, fb_ref, e_ref, a_ref, b_ref):
    frames, pairs, _, cols, c = x_ref.shape
    column, row, tcols = place()
    has_left, has_right = column > 0, column < tcols - 1
    even = lax.rem(column, 2) == 0
    upper = lax.rem(row, 2) == 0
    for f in range(frames):
        for r in range(2):
            lane = pl.ds(r * c, c)
            fa, fb = fa_ref[f, :, r], fb_ref[f, :, r]
            right = jnp.where(has_right, jnp.where(even, fa, fb), 0).astype(BF)
            left = jnp.where(has_left, jnp.where(even, fb, fa), 0).astype(BF)
            e_ref[f, :, 0:2, lane] = x_ref[f, :, r, cols - 2 :]
            e_ref[f, :, 2:4, lane] = right
            e_ref[f, :, 4:6, lane] = left
            e_ref[f, :, 6:8, lane] = x_ref[f, :, r, :2]
            top, bottom = x_ref[f, 0, r], x_ref[f, pairs - 1, r]
            a_ref[f, 0:cols, lane] = jnp.where(upper, bottom, top)
            b_ref[f, 0:cols, lane] = jnp.where(upper, top, bottom)
        top, bottom = e_ref[f, 0], e_ref[f, pairs - 1]
        a_ref[f, cols:, :] = jnp.where(upper, bottom, top)
        b_ref[f, cols:, :] = jnp.where(upper, top, bottom)


def ring_kernel(e_ref, va_ref, vb_ref, s_ref, w_ref, d_ref, r_ref, c_ref, m_ref, wide):
    frames, pairs, _, c2 = e_ref.shape
    n2 = r_ref.shape[3]
    cols = va_ref.shape[1] - 8
    upper = lax.rem(place()[1], 2) == 0
    _, row, _ = place()
    has_up, has_dn = row > 0, row < TROWS - 1
    spread(w_ref, wide)
    state = None
    rim = [None, None]
    for f in range(frames):
        keep = jnp.concatenate([d_ref[f : f + 1]] * 2, axis=-1).reshape(1, 1, n2)
        e = e_ref[f].reshape(pairs * 8, c2)
        high, low = dot(e, wide[:c2]), dot(e, wide[c2:])
        blank = jnp.zeros((8, 3 * n2), F32)
        y = jnp.concatenate([blank, high]) + jnp.concatenate([low, blank])
        y = gathered_edge(y, pairs + 1, n2)
        state = y if f == 0 else keep * state + y
        r_ref[f] = state
        va, vb = va_ref[f], vb_ref[f]
        near = (jnp.where(upper, vb, va), jnp.where(upper, va, vb))
        for side, there in enumerate((has_up, has_dn)):
            v = jnp.where(there, near[side], 0).astype(BF)
            y = dot(v, wide[c2:] if side else wide[:c2])
            mid = gathered(y[:cols], 1, cols, n2)
            end = gathered_edge(y[cols:], 1, n2)
            y = jnp.concatenate([mid, end], axis=1)
            rim[side] = y if f == 0 else keep * rim[side] + y
            c_ref[f, side : side + 1] = rim[side][:, :cols]
            at = side * pairs
            r_ref[f, at : at + 1] = r_ref[f, at : at + 1] + rim[side][:, cols:]
    last = frames - 1
    whole, ends = merged(s_ref, r_ref, c_ref, last)
    m_ref[:, :cols] = whole.astype(BF)
    m_ref[:, cols:] = ends.astype(BF)


def merged(s_ref, r_ref, c_ref, f):
    rim = c_ref[f]
    body = s_ref[f]
    n, cols, n2 = body.shape
    body = jnp.concatenate([body[:1] + rim[:1], body[1 : n - 1], body[n - 1 :] + rim[1:]])
    ends = r_ref[f]
    col = lax.broadcasted_iota(jnp.int32, ends.shape, 1)
    first = body[:, :8] + jnp.where(col == 0, pltpu.roll(ends, 2, 1), 0.0)
    final = body[:, cols - 8 :] + jnp.where(col == 7, pltpu.roll(ends, 6, 1), 0.0)
    return jnp.concatenate([first, body[:, 8 : cols - 8], final], axis=1), ends


def read_kernel(
    s_ref, r_ref, c_ref, m_ref, w_ref, d_ref, skip_ref, x_ref, o_ref, wide, held, ends_held, out, sems
):
    frames, pairs, _, cols, c = x_ref.shape
    n2 = s_ref.shape[3]
    spread(w_ref, wide)
    column, row, tcols = place()
    later = (lax.axis_index("tm") > 0).astype(F32)
    has_up, has_dn = row > 0, row < TROWS - 1
    has_left, has_right = column > 0, column < tcols - 1
    gain = jnp.concatenate([skip_ref[...]] * 2, axis=-1)
    factor = jnp.full((1, n2), 1.0, F32) * later
    lane = lax.broadcasted_iota(jnp.int32, (1, 1, n2), 2)
    copies = []
    for f in range(frames):
        factor = factor * jnp.concatenate([d_ref[f : f + 1]] * 2, axis=-1)
        body, ends = merged(s_ref, r_ref, c_ref, f)
        far = factor.reshape(1, 1, n2)
        body = body + far * m_ref[:, :cols].astype(F32)
        ends = ends + far * m_ref[:, cols:].astype(F32)
        col = lax.broadcasted_iota(jnp.int32, ends.shape, 1)
        ends = jnp.where(((col == 2) & has_right) | ((col == 5) & has_left), ends, 0.0)
        for value, ref in ((body, held), (ends, ends_held)):
            ref[...] = value.astype(BF)
            ref[0:1] = jnp.where(has_up | (lane >= n2 // 2), value[0:1], 0.0).astype(BF)
            ref[pairs : pairs + 1] = jnp.where(
                has_dn | (lane < n2 // 2), value[pairs : pairs + 1], 0.0
            ).astype(BF)
        for p in range(0, pairs, BLOCK):
            n = min(BLOCK, pairs - p)
            y = dot(held[p : p + n].reshape(n * cols, n2), wide[:n2])
            y = y + dot(held[p + 1 : p + 1 + n].reshape(n * cols, n2), wide[n2:])
            y = gathered(y, n, cols, n2)
            e = dot(ends_held[p : p + n].reshape(n * 8, n2), wide[:n2])
            e = e + dot(ends_held[p + 1 : p + 1 + n].reshape(n * 8, n2), wide[n2:])
            e = e.reshape(n, 8, 3 * n2)
            col = lax.broadcasted_iota(jnp.int32, (n, 8, n2), 1)
            first = y[:, :8] + jnp.where(col == 0, pltpu.roll(e[:, :, :n2], 3, 1), 0.0)
            final = y[:, cols - 8 :] + jnp.where(col == 7, pltpu.roll(e[:, :, 2 * n2 :], 5, 1), 0.0)
            y = jnp.concatenate([first, y[:, 8 : cols - 8], final], axis=1)
            half = n2 // 2
            for r in range(2):
                v = y[:, :, r * half : (r + 1) * half]
                v = v + gain[:, :half].reshape(1, 1, half) * x_ref[f, p : p + n, r].astype(F32)
                out[f, p : p + n, r] = v.astype(BF)
        copy = pltpu.make_async_copy(out.at[f], o_ref.at[f], sems.at[f])
        copy.start()
        copies.append(copy)
    for copy in copies:
        copy.wait()


def call(body, outs, ins, scratch=(), in_specs=None, out_specs=None, name=None, limit=LIMIT):
    return pl.pallas_call(
        body,
        out_shape=outs,
        in_specs=in_specs or [VM] * len(ins),
        out_specs=out_specs if out_specs is not None else jax.tree.map(lambda _: VM, outs),
        scratch_shapes=list(scratch),
        compiler_params=pltpu.CompilerParams(vmem_limit_bytes=limit),
        name=name,
    )(*ins)


def per_device(frames, w_in, w_out, decay, skip):
    shape = jax.ShapeDtypeStruct
    count, _, rows, cols, c = frames.shape
    n2 = 2 * w_in.shape[3]
    pairs = rows // 2
    video = frames.reshape(count, pairs, 2, cols, c)
    side = shape((count, pairs, 2, 2, c), BF)
    across = shape((count, cols + 8, 2 * c), BF)
    here, side_a, side_b = call(
        pack_kernel,
        (shape(video.shape, BF), side, side),
        (pltpu.with_memory_space_constraint(video, pltpu.HBM),),
        [pltpu.SemaphoreType.DMA((count,))],
        in_specs=[pl.BlockSpec(memory_space=pltpu.HBM)],
        name="pack",
        limit=LIMIT,
    )
    from_a = swapped(side_a, True, 0)
    from_b = swapped(side_b, True, 1)
    local = call(
        main_kernel,
        shape((count, pairs + 1, cols, n2), F32),
        (here, w_in, decay),
        [pltpu.VMEM((4 * c, 3 * n2), BF)],
        name="main",
    )
    from_a, from_b, local = lax.optimization_barrier((from_a, from_b, local))
    edge, row_a, row_b = call(
        edge_kernel,
        (shape((count, pairs, 8, 2 * c), BF), across, across),
        (here, from_a, from_b),
        name="edge",
    )
    rows_a = swapped(row_a, False, 0)
    rows_b = swapped(row_b, False, 1)
    ends, rim, message = call(
        ring_kernel,
        (
            shape((count, pairs + 1, 8, n2), F32),
            shape((count, 2, cols, n2), F32),
            shape((pairs + 1, cols + 8, n2), BF),
        ),
        (edge, rows_a, rows_b, local, w_in, decay),
        [pltpu.VMEM((4 * c, 3 * n2), BF)],
        name="ring",
    )
    groups = lax.axis_size("tm")
    before = lax.ppermute(message, "tm", [(i, (i + 1) % groups) for i in range(groups)])
    mixed = call(
        read_kernel,
        shape((count, pairs, 2, cols, c), BF),
        (local, ends, rim, before, w_out, decay, skip.reshape(1, c), here),
        [
            pltpu.VMEM((2 * n2, 3 * 2 * c), BF),
            pltpu.VMEM((pairs + 1, cols, n2), BF),
            pltpu.VMEM((pairs + 1, 8, n2), BF),
            pltpu.VMEM((count, pairs, 2, cols, c), BF),
            pltpu.SemaphoreType.DMA((count,)),
        ],
        out_specs=ANY,
        name="read",
    )
    return mixed.reshape(count, 1, rows, cols, c)


def solution(mesh):
    return jax.shard_map(
        per_device,
        mesh=mesh,
        in_specs=(P("tm", "tile", None, None, None), P(), P(), P("tm", None), P()),
        out_specs=P("tm", "tile", None, None, None),
        check_vma=False,
    )
```

```python
import functools

import jax
import jax.numpy as jnp
from jax import lax
from jax.experimental import pallas as pl
from jax.experimental.pallas import tpu as pltpu
from jax.sharding import PartitionSpec as P

TROWS = 4
BF = jnp.bfloat16
F32 = jnp.float32
LIMIT = 24 << 20
BLOCK = 16
VM = pl.BlockSpec(memory_space=pltpu.VMEM)
ANY = pl.BlockSpec(memory_space=pl.ANY)


def swapped(value, across, first):
    count = lax.axis_size("tile")
    tcols = count // TROWS
    pairs = []
    for number in range(count):
        row, column = divmod(number, tcols)
        at, size = (column, tcols) if across else (row, TROWS)
        other = at + 1 if at >= first and (at - first) % 2 == 0 else at - 1
        if not first <= other < size:
            other = at
        there = row * tcols + other if across else other * tcols + column
        pairs.append(((number + 1) % count, (there + 1) % count))
    return lax.ppermute(value, "tile", pairs)


def onward(value):
    groups = lax.axis_size("tm")
    return lax.ppermute(value, "tm", [(i, (i + 1) % groups) for i in range(groups)])


def place():
    count = lax.axis_size("tile")
    tcols = count // TROWS
    number = lax.rem(lax.axis_index("tile") + count - 1, count)
    return lax.rem(number, tcols), lax.div(number, tcols), tcols


def dot(a, b):
    return jnp.dot(a, b, preferred_element_type=F32)


def spread(w_ref, wide):
    c, n = w_ref.shape[2:]
    zero = jnp.zeros((c, n), BF)
    for tap in range(3):
        for row in range(4):
            for out in range(2):
                at = tap * 2 * n + out * n
                k = row - out
                wide[row * c : (row + 1) * c, at : at + n] = w_ref[k, tap] if 0 <= k <= 2 else zero


def gathered(y, pairs, cols, n2):
    y = y.reshape(pairs, cols, 3 * n2)
    left, mid, right = y[:, :, :n2], y[:, :, n2 : 2 * n2], y[:, :, 2 * n2 :]
    col = lax.broadcasted_iota(jnp.int32, mid.shape, 1)
    left = jnp.where(col > 0, pltpu.roll(left, 1, 1), 0.0)
    right = jnp.where(col < cols - 1, pltpu.roll(right, cols - 1, 1), 0.0)
    return mid + left + right


def gathered_edge(y, pairs, n2):
    y = y.reshape(pairs, 8, 3 * n2)
    left, mid, right = y[:, :, :n2], y[:, :, n2 : 2 * n2], y[:, :, 2 * n2 :]
    col = lax.broadcasted_iota(jnp.int32, mid.shape, 1)
    full = (col == 2) | (col == 5)
    left = jnp.where(full | (col == 6), pltpu.roll(left, 1, 1), 0.0)
    right = jnp.where(full | (col == 1), pltpu.roll(right, 7, 1), 0.0)
    return jnp.where(full, mid, 0.0) + left + right


def blocks(pairs):
    return [(q, min(BLOCK, pairs - q)) for q in range(1, pairs, BLOCK)]


def main_kernel(x_ref, w_ref, d_ref, s_ref, m_ref, wide):
    frames, pairs, _, cols, c = x_ref.shape
    n2 = s_ref.shape[3]
    spread(w_ref, wide)

    def rows(f, p, n):
        return jnp.concatenate(
            [x_ref[f, p : p + n, r].reshape(n * cols, c) for r in range(2)], axis=-1
        )

    for q, n in [(0, 1), *blocks(pairs), (pairs, 1)]:
        state = None
        for f in range(frames):
            y = None
            if q > 0:
                y = dot(rows(f, q - 1, n), wide[: 2 * c])
            if q < pairs:
                low = dot(rows(f, q, n), wide[2 * c :])
                y = low if y is None else y + low
            y = gathered(y, n, cols, n2)
            keep = jnp.concatenate([d_ref[f : f + 1]] * 2, axis=-1).reshape(1, 1, n2)
            state = y if f == 0 else keep * state + y
            s_ref[f, q : q + n] = state
        m_ref[q : q + n] = state.astype(BF)


def pack_kernel(f_ref, x_ref, a_ref, b_ref, sems):
    frames, _, _, cols, _ = x_ref.shape
    column, _, _ = place()
    even = lax.rem(column, 2) == 0
    copies = [
        pltpu.make_async_copy(f_ref.at[f], x_ref.at[f], sems.at[f]) for f in range(frames)
    ]
    for copy in copies:
        copy.start()
    for f, copy in enumerate(copies):
        copy.wait()
        low, high = x_ref[f, :, :, :2], x_ref[f, :, :, cols - 2 :]
        a_ref[f] = jnp.where(even, high, low)
        b_ref[f] = jnp.where(even, low, high)


def edge_kernel(x_ref, fa_ref, fb_ref, e_ref, a_ref, b_ref):
    frames, pairs, _, cols, c = x_ref.shape
    column, row, tcols = place()
    has_left, has_right = column > 0, column < tcols - 1
    even = lax.rem(column, 2) == 0
    upper = lax.rem(row, 2) == 0
    for f in range(frames):
        for r in range(2):
            lane = pl.ds(r * c, c)
            fa, fb = fa_ref[f, :, r], fb_ref[f, :, r]
            right = jnp.where(has_right, jnp.where(even, fa, fb), 0).astype(BF)
            left = jnp.where(has_left, jnp.where(even, fb, fa), 0).astype(BF)
            e_ref[f, :, 0:2, lane] = x_ref[f, :, r, cols - 2 :]
            e_ref[f, :, 2:4, lane] = right
            e_ref[f, :, 4:6, lane] = left
            e_ref[f, :, 6:8, lane] = x_ref[f, :, r, :2]
            top, bottom = x_ref[f, 0, r], x_ref[f, pairs - 1, r]
            a_ref[f, 0:cols, lane] = jnp.where(upper, bottom, top)
            b_ref[f, 0:cols, lane] = jnp.where(upper, top, bottom)
        top, bottom = e_ref[f, 0], e_ref[f, pairs - 1]
        a_ref[f, cols:, :] = jnp.where(upper, bottom, top)
        b_ref[f, cols:, :] = jnp.where(upper, top, bottom)


def twice(ref, f):
    return jnp.concatenate([ref[f : f + 1]] * 2, axis=-1)


def inner_kernel(e_ref, w_ref, d_ref, r_ref, wide):
    frames, pairs, _, c2 = e_ref.shape
    n2 = r_ref.shape[3]
    spread(w_ref, wide)
    state = None
    blank = jnp.zeros((8, 3 * n2), F32)
    for f in range(frames):
        e = e_ref[f].reshape(pairs * 8, c2)
        high, low = dot(e, wide[:c2]), dot(e, wide[c2:])
        y = jnp.concatenate([blank, high]) + jnp.concatenate([low, blank])
        y = gathered_edge(y, pairs + 1, n2)
        state = y if f == 0 else twice(d_ref, f).reshape(1, 1, n2) * state + y
        r_ref[f] = state


def ring_kernel(va_ref, vb_ref, p_ref, w_ref, d_ref, r_ref, c_ref, m_ref, wide):
    frames, size, c2 = va_ref.shape
    pairs, n2 = r_ref.shape[1] - 1, r_ref.shape[3]
    cols = size - 8
    _, row, _ = place()
    upper = lax.rem(row, 2) == 0
    spread(w_ref, wide)
    last = frames - 1
    r_ref[...] = p_ref[...]
    for side, there in enumerate((row > 0, row < TROWS - 1)):
        take_a = upper == (side == 1)
        v = jnp.where(there, jnp.where(take_a, va_ref[...], vb_ref[...]), 0).astype(BF)
        y = dot(v.reshape(frames * size, c2), wide[c2:] if side else wide[:c2])
        y = y.reshape(frames, size, 3 * n2)
        mid = gathered(y[:, :cols], frames, cols, n2)
        end = gathered_edge(y[:, cols:], frames, n2)
        y = jnp.concatenate([mid, end], axis=1)
        at = side * pairs
        state = None
        for f in range(frames):
            state = y[f] if f == 0 else twice(d_ref, f) * state + y[f]
            c_ref[f, side] = state[:cols]
            r_ref[f, at] = p_ref[f, at] + state[cols:]
        for k in range(cols // 8):
            m_ref[pairs + 1 + side * (cols // 8) + k] = state[8 * k : 8 * k + 8].astype(BF)
    m_ref[: pairs + 1] = r_ref[last].astype(BF)


def row_masked(value, q, pairs):
    _, row, _ = place()
    _, _, n2 = value.shape
    pair = lax.broadcasted_iota(jnp.int32, value.shape, 0) + q
    lane = lax.broadcasted_iota(jnp.int32, value.shape, 2)
    off = ((pair == 0) & (lane < n2 // 2) & (row == 0)) | (
        (pair == pairs) & (lane >= n2 // 2) & (row == TROWS - 1)
    )
    return jnp.where(off, 0.0, value)


def read_kernel(first, *refs):
    s_ref, m_ref, w_ref, d_ref, skip_ref, x_ref = refs[:6]
    o_ref, side_ref, rim_ref, wide, held, out, sems = refs[-7:]
    _, pairs, _, cols, _ = x_ref.shape
    n2 = s_ref.shape[3]
    half = n2 // 2
    spread(w_ref, wide)
    later = (lax.axis_index("tm") > 0).astype(F32)
    gain = skip_ref[...].reshape(1, 1, half)
    factor = jnp.full((1, n2), 1.0, F32) * later
    for f in range(first):
        factor = factor * twice(d_ref, f)
    copies = []
    for i in range(side_ref.shape[0]):
        f = first + i
        factor = factor * twice(d_ref, f)
        body = s_ref[f] + factor.reshape(1, 1, n2) * m_ref[...].astype(F32)
        held[...] = body.astype(BF)
        held[0:1] = row_masked(body[0:1], 0, pairs).astype(BF)
        held[pairs:] = row_masked(body[pairs:], pairs, pairs).astype(BF)
        for p in range(0, pairs, BLOCK):
            n = min(BLOCK, pairs - p)
            y = dot(held[p : p + n].reshape(n * cols, n2), wide[:n2])
            y = y + dot(held[p + 1 : p + 1 + n].reshape(n * cols, n2), wide[n2:])
            y = gathered(y, n, cols, n2)
            for r in range(2):
                lane = pl.ds(r * half, half)
                v = y[:, :, r * half : (r + 1) * half]
                v = v + gain * x_ref[f, p : p + n, r].astype(F32)
                out[i, p : p + n, r] = v[:, 8 : cols - 8].astype(BF)
                side_ref[i, p : p + n, 0:8, lane] = v[:, :8]
                side_ref[i, p : p + n, 8:16, lane] = v[:, cols - 8 :]
                if p == 0:
                    rim_ref[i, 0, :, lane] = v[0, 8 : cols - 8]
                if p + n == pairs:
                    rim_ref[i, 1, :, lane] = v[n - 1, 8 : cols - 8]
        copy = pltpu.make_async_copy(
            out.at[i], o_ref.at[f, :, :, pl.ds(8, cols - 16)], sems.at[i]
        )
        copy.start()
        copies.append(copy)
    for copy in copies:
        copy.wait()


def last_kernel(r_ref, c_ref, m_ref, w_ref, d_ref, *refs):
    count = (len(refs) - 7) // 2
    sides, rims = refs[:count], refs[count : 2 * count]
    o_ref, wide, held, left, right, rows, sems = refs[2 * count :][-7:]
    frames, rest, _, n2 = r_ref.shape
    pairs, half = rest - 1, n2 // 2
    cols = c_ref.shape[2]
    spread(w_ref, wide)
    column, _, tcols = place()
    later = (lax.axis_index("tm") > 0).astype(F32)
    factor = jnp.full((1, n2), 1.0, F32) * later
    ends, rim = [], []
    for f in range(frames):
        factor = factor * twice(d_ref, f)
        far = factor.reshape(1, 1, n2)
        e = r_ref[f] + far * m_ref[: pairs + 1].astype(F32)
        col = lax.broadcasted_iota(jnp.int32, e.shape, 1)
        e = jnp.where(((col == 2) & (column == tcols - 1)) | ((col == 5) & (column == 0)), 0.0, e)
        ends.append(row_masked(e, 0, pairs))
        more = m_ref[pairs + 1 :].astype(F32).reshape(2, cols, n2)
        rim.append(row_masked(c_ref[f] + far * more, 0, 1).astype(BF))
    for f in range(0, frames, 2):
        e = ends[f]
        if f + 1 < frames:
            col = lax.broadcasted_iota(jnp.int32, e.shape, 1)
            own = (col == 1) | (col == 2) | (col == 5) | (col == 6)
            e = jnp.where(own, e, pltpu.roll(ends[f + 1], 2, 1))
        held[f // 2] = e.astype(BF)
    edge_rows = []
    for side in range(2):
        v = jnp.stack([rim[f][side] for f in range(frames)]).reshape(frames * cols, n2)
        y = dot(v, wide[n2:] if side else wide[:n2])
        edge_rows.append(gathered(y, frames, cols, n2))
    copies = []
    for f in range(frames):
        if f % 2 == 0:
            e = held[f // 2]
            y = dot(e[:pairs].reshape(pairs * 8, n2), wide[:n2])
            y = y + dot(e[1:].reshape(pairs * 8, n2), wide[n2:])
            y = y.reshape(pairs, 8, 3 * n2)
            y0, y1, y2 = y[:, :, :n2], y[:, :, n2 : 2 * n2], y[:, :, 2 * n2 :]
        col = lax.broadcasted_iota(jnp.int32, (pairs, 8, n2), 1)
        a, b, d, g = (3, 2, 5, 6) if f % 2 == 0 else (1, 0, 3, 4)
        near = jnp.where(col < 2, pltpu.roll(y0, a, 1), 0.0)
        near = near + jnp.where(col == 0, pltpu.roll(y1, b, 1) if b else y1, 0.0)
        far = jnp.where(col >= 6, pltpu.roll(y2, d, 1), 0.0)
        far = far + jnp.where(col == 7, pltpu.roll(y1, g, 1), 0.0)
        which, i = divmod(f, sides[0].shape[0])
        for at, part, ref, base in ((0, near, left, 0), (8, far, right, cols - 8)):
            total = sides[which][i, :, at : at + 8] + part
            for r in range(2):
                ref[f, :, r] = total[:, :, r * half : (r + 1) * half].astype(BF)
                lane = slice(r * half, (r + 1) * half)
                top = total[:1, :, lane] + edge_rows[0][f : f + 1, base : base + 8, lane]
                low = total[pairs - 1 :, :, lane] + edge_rows[1][f : f + 1, base : base + 8, lane]
                ref[f, 0:1, r] = top.astype(BF)
                ref[f, pairs - 1 :, r] = low.astype(BF)
        for k in range(2):
            v = rims[which][i, k] + edge_rows[k][f, 8 : cols - 8]
            for r in range(2):
                rows[f, k, r] = v[:, r * half : (r + 1) * half].astype(BF)
        ends_of = ((0, 0), (pairs - 1, 1))
        mine = [
            (left.at[f], o_ref.at[f, :, :, pl.ds(0, 8)]),
            (right.at[f], o_ref.at[f, :, :, pl.ds(cols - 8, 8)]),
            *((rows.at[f, k], o_ref.at[f, p, :, pl.ds(8, cols - 16)]) for p, k in ends_of),
        ]
        for k, (source, target) in enumerate(mine):
            copy = pltpu.make_async_copy(source, target, sems.at[f, k])
            copy.start()
            copies.append(copy)
    for copy in copies:
        copy.wait()


def call(body, outs, ins, scratch=(), in_specs=None, out_specs=None, aliases=None):
    return pl.pallas_call(
        body,
        out_shape=outs,
        in_specs=in_specs or [VM] * len(ins),
        out_specs=out_specs if out_specs is not None else jax.tree.map(lambda _: VM, outs),
        scratch_shapes=list(scratch),
        compiler_params=pltpu.CompilerParams(vmem_limit_bytes=LIMIT),
        input_output_aliases=aliases or {},
    )(*ins)


def per_device(frames, w_in, w_out, decay, skip):
    shape = jax.ShapeDtypeStruct
    count, _, rows, cols, c = frames.shape
    n2 = 2 * w_in.shape[3]
    pairs = rows // 2
    video = frames.reshape(count, pairs, 2, cols, c)
    side = shape((count, pairs, 2, 2, c), BF)
    across = shape((count, cols + 8, 2 * c), BF)
    here, side_a, side_b = call(
        pack_kernel,
        (shape(video.shape, BF), side, side),
        (pltpu.with_memory_space_constraint(video, pltpu.HBM),),
        [pltpu.SemaphoreType.DMA((count,))],
        in_specs=[pl.BlockSpec(memory_space=pltpu.HBM)],
    )
    from_a = swapped(side_a, True, 0)
    from_b = swapped(side_b, True, 1)
    wide_in = pltpu.VMEM((4 * c, 3 * n2), BF)
    wide_out = pltpu.VMEM((2 * n2, 3 * 2 * c), BF)
    local, message = call(
        main_kernel,
        (shape((count, pairs + 1, cols, n2), F32), shape((pairs + 1, cols, n2), BF)),
        (here, w_in, decay),
        [wide_in],
    )
    before = onward(message)
    from_a, from_b, local = lax.optimization_barrier((from_a, from_b, local))
    edge, row_a, row_b = call(
        edge_kernel, (shape((count, pairs, 8, 2 * c), BF), across, across), (here, from_a, from_b)
    )
    rows_a = swapped(row_a, False, 0)
    rows_b = swapped(row_b, False, 1)
    edge_states = shape((count, pairs + 1, 8, n2), F32)
    edge, local, before = lax.optimization_barrier((edge, local, before))
    partial = call(inner_kernel, edge_states, (edge, w_in, decay), [wide_in])
    part = count // 2

    def read(first, mixed, local):
        given = (local, before, w_out, decay, skip.reshape(1, c), here)
        return call(
            functools.partial(read_kernel, first),
            (
                shape(video.shape, BF),
                shape((part, pairs, 16, n2), F32),
                shape((part, 2, cols - 16, n2), F32),
            ),
            given if mixed is None else (*given, mixed),
            [
                wide_out,
                pltpu.VMEM((pairs + 1, cols, n2), BF),
                pltpu.VMEM((part, pairs, 2, cols - 16, c), BF),
                pltpu.SemaphoreType.DMA((part,)),
            ],
            in_specs=[VM] * len(given) + ([] if mixed is None else [ANY]),
            out_specs=(ANY, VM, VM),
            aliases={} if mixed is None else {len(given): 0},
        )

    mixed, side_0, rim_0 = read(0, None, local)
    rows_a, rows_b, partial, side_0, local = lax.optimization_barrier(
        (rows_a, rows_b, partial, side_0, local)
    )
    ends, rim, message = call(
        ring_kernel,
        (edge_states, shape((count, 2, cols, n2), F32), shape((pairs + 1 + cols // 4, 8, n2), BF)),
        (rows_a, rows_b, partial, w_in, decay),
        [wide_in],
    )
    ring_before = onward(message)
    ends, local = lax.optimization_barrier((ends, local))
    mixed, side_1, rim_1 = read(part, mixed, local)
    ring_before, side_1 = lax.optimization_barrier((ring_before, side_1))
    given = (ends, rim, ring_before, w_out, decay, side_0, side_1, rim_0, rim_1)
    mixed = call(
        last_kernel,
        shape(video.shape, BF),
        (*given, mixed),
        [
            wide_out,
            pltpu.VMEM(((count + 1) // 2, pairs + 1, 8, n2), BF),
            pltpu.VMEM((count, pairs, 2, 8, c), BF),
            pltpu.VMEM((count, pairs, 2, 8, c), BF),
            pltpu.VMEM((count, 2, 2, cols - 16, c), BF),
            pltpu.SemaphoreType.DMA((count, 4)),
        ],
        in_specs=[VM] * len(given) + [ANY],
        out_specs=ANY,
        aliases={len(given): 0},
    )
    return mixed.reshape(count, 1, rows, cols, c)


def solution(mesh):
    return jax.shard_map(
        per_device,
        mesh=mesh,
        in_specs=(P("tm", "tile", None, None, None), P(), P(), P("tm", None), P()),
        out_specs=P("tm", "tile", None, None, None),
        check_vma=False,
    )
```

```python
import functools

import jax
import jax.numpy as jnp
from jax import lax
from jax.experimental import pallas as pl
from jax.experimental.pallas import tpu as pltpu
from jax.sharding import PartitionSpec as P

TROWS = 4
BF = jnp.bfloat16
F32 = jnp.float32
LIMIT = 24 << 20
BLOCK = 16
VM = pl.BlockSpec(memory_space=pltpu.VMEM)
ANY = pl.BlockSpec(memory_space=pl.ANY)


def swapped(value, across, first):
    count = lax.axis_size("tile")
    tcols = count // TROWS
    pairs = []
    for number in range(count):
        row, column = divmod(number, tcols)
        at, size = (column, tcols) if across else (row, TROWS)
        other = at + 1 if at >= first and (at - first) % 2 == 0 else at - 1
        if not first <= other < size:
            other = at
        there = row * tcols + other if across else other * tcols + column
        pairs.append(((number + 1) % count, (there + 1) % count))
    return lax.ppermute(value, "tile", pairs)


def onward(value):
    groups = lax.axis_size("tm")
    return lax.ppermute(value, "tm", [(i, (i + 1) % groups) for i in range(groups)])


def place():
    count = lax.axis_size("tile")
    tcols = count // TROWS
    number = lax.rem(lax.axis_index("tile") + count - 1, count)
    return lax.rem(number, tcols), lax.div(number, tcols), tcols


def dot(a, b):
    return jnp.dot(a, b, preferred_element_type=F32)


def spread(w_ref, wide):
    c, n = w_ref.shape[2:]
    zero = jnp.zeros((c, n), BF)
    for tap in range(3):
        for row in range(4):
            for out in range(2):
                at = tap * 2 * n + out * n
                k = row - out
                wide[row * c : (row + 1) * c, at : at + n] = w_ref[k, tap] if 0 <= k <= 2 else zero


def gathered(y, pairs, cols, n2):
    y = y.reshape(pairs, cols, 3 * n2)
    left, mid, right = y[:, :, :n2], y[:, :, n2 : 2 * n2], y[:, :, 2 * n2 :]
    col = lax.broadcasted_iota(jnp.int32, mid.shape, 1)
    left = jnp.where(col > 0, pltpu.roll(left, 1, 1), 0.0)
    right = jnp.where(col < cols - 1, pltpu.roll(right, cols - 1, 1), 0.0)
    return mid + left + right


def gathered_edge(y, pairs, n2):
    y = y.reshape(pairs, 8, 3 * n2)
    left, mid, right = y[:, :, :n2], y[:, :, n2 : 2 * n2], y[:, :, 2 * n2 :]
    col = lax.broadcasted_iota(jnp.int32, mid.shape, 1)
    full = (col == 2) | (col == 5)
    left = jnp.where(full | (col == 6), pltpu.roll(left, 1, 1), 0.0)
    right = jnp.where(full | (col == 1), pltpu.roll(right, 7, 1), 0.0)
    return jnp.where(full, mid, 0.0) + left + right


def blocks(pairs):
    every = [(0, 1), *((q, min(BLOCK, pairs - q)) for q in range(1, pairs, BLOCK)), (pairs, 1)]
    cut = pairs // 2 + 1
    return [b for b in every if b[0] + b[1] <= cut], [b for b in every if b[0] + b[1] > cut]


def ahead():
    return lax.axis_index("tile") == 0


def own_states(x_ref, wide, d_ref, s_ref, m_ref, chosen):
    frames, pairs, _, cols, c = x_ref.shape
    n2 = s_ref.shape[3]

    def rows(f, p, n):
        return jnp.concatenate(
            [x_ref[f, p : p + n, r].reshape(n * cols, c) for r in range(2)], axis=-1
        )

    for q, n in chosen:
        state = None
        for f in range(frames):
            y = None
            if q > 0:
                y = dot(rows(f, q - 1, n), wide[: 2 * c])
            if q < pairs:
                low = dot(rows(f, q, n), wide[2 * c :])
                y = low if y is None else y + low
            y = gathered(y, n, cols, n2)
            state = y if f == 0 else twice(d_ref, f).reshape(1, 1, n2) * state + y
            s_ref[f, q : q + n] = state
        if m_ref is not None:
            m_ref[q : q + n] = state.astype(BF)


def early_kernel(x_ref, w_ref, d_ref, s_ref, wide):
    @pl.when(ahead())
    def _():
        spread(w_ref, wide)
        own_states(x_ref, wide, d_ref, s_ref, None, blocks(x_ref.shape[1])[0])


def main_kernel(x_ref, w_ref, d_ref, p_ref, s_ref, m_ref, wide):
    head, tail = blocks(x_ref.shape[1])
    spread(w_ref, wide)

    @pl.when(jnp.logical_not(ahead()))
    def _():
        own_states(x_ref, wide, d_ref, s_ref, m_ref, head)

    own_states(x_ref, wide, d_ref, s_ref, m_ref, tail)

    @pl.when(ahead())
    def _():
        done = p_ref.shape[1]
        s_ref[:, :done] = p_ref[...]
        m_ref[:done] = p_ref[p_ref.shape[0] - 1].astype(BF)


def pack_kernel(f_ref, x_ref, a_ref, b_ref, sems):
    frames, _, _, cols, _ = x_ref.shape
    column, _, _ = place()
    even = lax.rem(column, 2) == 0
    copies = [
        pltpu.make_async_copy(f_ref.at[f], x_ref.at[f], sems.at[f]) for f in range(frames)
    ]
    for copy in copies:
        copy.start()
    for f, copy in enumerate(copies):
        copy.wait()
        low, high = x_ref[f, :, :, :2], x_ref[f, :, :, cols - 2 :]
        a_ref[f] = jnp.where(even, high, low)
        b_ref[f] = jnp.where(even, low, high)


def group_of(x_ref, fa_ref, fb_ref, f, p, e_ref, at):
    _, _, _, cols, c = x_ref.shape
    column, _, tcols = place()
    even = lax.rem(column, 2) == 0
    for r in range(2):
        lane = pl.ds(r * c, c)
        fa, fb = fa_ref[f, p, r], fb_ref[f, p, r]
        right = jnp.where(column < tcols - 1, jnp.where(even, fa, fb), 0).astype(BF)
        left = jnp.where(column > 0, jnp.where(even, fb, fa), 0).astype(BF)
        e_ref[at, :, 0:2, lane] = x_ref[f, p, r, cols - 2 :]
        e_ref[at, :, 2:4, lane] = right
        e_ref[at, :, 4:6, lane] = left
        e_ref[at, :, 6:8, lane] = x_ref[f, p, r, :2]


def edge_kernel(x_ref, fa_ref, fb_ref, a_ref, b_ref, e_ref):
    frames, pairs, _, cols, c = x_ref.shape
    _, row, _ = place()
    upper = lax.rem(row, 2) == 0
    for f in range(frames):
        for k, p in enumerate((0, pairs - 1)):
            group_of(x_ref, fa_ref, fb_ref, f, slice(p, p + 1), e_ref, 2 * f + k)
        for r in range(2):
            lane = pl.ds(r * c, c)
            top, bottom = x_ref[f, 0, r], x_ref[f, pairs - 1, r]
            a_ref[f, 0:cols, lane] = jnp.where(upper, bottom, top)
            b_ref[f, 0:cols, lane] = jnp.where(upper, top, bottom)
        top, bottom = e_ref[2 * f, 0], e_ref[2 * f + 1, 0]
        a_ref[f, cols:, :] = jnp.where(upper, bottom, top)
        b_ref[f, cols:, :] = jnp.where(upper, top, bottom)


def twice(ref, f):
    return jnp.concatenate([ref[f : f + 1]] * 2, axis=-1)


def inner_kernel(x_ref, fa_ref, fb_ref, wide, d_ref, r_ref, e_ref):
    frames, pairs, _, c2 = e_ref.shape
    n2 = r_ref.shape[3]
    state = None
    blank = jnp.zeros((8, 3 * n2), F32)
    for f in range(frames):
        group_of(x_ref, fa_ref, fb_ref, f, slice(None), e_ref, f)
        e = e_ref[f].reshape(pairs * 8, c2)
        high, low = dot(e, wide[:c2]), dot(e, wide[c2:])
        y = jnp.concatenate([blank, high]) + jnp.concatenate([low, blank])
        y = gathered_edge(y, pairs + 1, n2)
        state = y if f == 0 else twice(d_ref, f).reshape(1, 1, n2) * state + y
        r_ref[f] = state


def ring_kernel(va_ref, vb_ref, p_ref, wide, d_ref, r_ref, c_ref, m_ref):
    frames, size, c2 = va_ref.shape
    pairs, n2 = r_ref.shape[1] - 1, r_ref.shape[3]
    cols = size - 8
    _, row, _ = place()
    upper = lax.rem(row, 2) == 0
    last = frames - 1
    r_ref[...] = p_ref[...]
    for side, there in enumerate((row > 0, row < TROWS - 1)):
        take_a = upper == (side == 1)
        v = jnp.where(there, jnp.where(take_a, va_ref[...], vb_ref[...]), 0).astype(BF)
        y = dot(v.reshape(frames * size, c2), wide[c2:] if side else wide[:c2])
        y = y.reshape(frames, size, 3 * n2)
        mid = gathered(y[:, :cols], frames, cols, n2)
        end = gathered_edge(y[:, cols:], frames, n2)
        y = jnp.concatenate([mid, end], axis=1)
        at = side * pairs
        state = None
        for f in range(frames):
            state = y[f] if f == 0 else twice(d_ref, f) * state + y[f]
            c_ref[f, side] = state[:cols]
            r_ref[f, at] = p_ref[f, at] + state[cols:]
        for k in range(cols // 8):
            m_ref[pairs + 1 + side * (cols // 8) + k] = state[8 * k : 8 * k + 8].astype(BF)
    m_ref[: pairs + 1] = r_ref[last].astype(BF)


def row_masked(value, q, pairs):
    _, row, _ = place()
    _, _, n2 = value.shape
    pair = lax.broadcasted_iota(jnp.int32, value.shape, 0) + q
    lane = lax.broadcasted_iota(jnp.int32, value.shape, 2)
    off = ((pair == 0) & (lane < n2 // 2) & (row == 0)) | (
        (pair == pairs) & (lane >= n2 // 2) & (row == TROWS - 1)
    )
    return jnp.where(off, 0.0, value)


def read_kernel(first, *refs):
    s_ref, m_ref, w_ref, d_ref, skip_ref, x_ref = refs[:6]
    if first == 0:
        wide = refs[-4]
        spread(w_ref, wide)
        o_ref, side_ref, rim_ref = refs[-7:-4]
    else:
        wide = w_ref
        o_ref, side_ref, rim_ref = refs[-6:-3]
    held, out, sems = refs[-3:]
    _, pairs, _, cols, _ = x_ref.shape
    n2 = s_ref.shape[3]
    half = n2 // 2
    later = (lax.axis_index("tm") > 0).astype(F32)
    gain = skip_ref[...].reshape(1, 1, half)
    factor = jnp.full((1, n2), 1.0, F32) * later
    for f in range(first):
        factor = factor * twice(d_ref, f)
    copies = []
    for i in range(side_ref.shape[0]):
        f = first + i
        factor = factor * twice(d_ref, f)
        body = s_ref[f] + factor.reshape(1, 1, n2) * m_ref[...].astype(F32)
        held[...] = body.astype(BF)
        held[0:1] = row_masked(body[0:1], 0, pairs).astype(BF)
        held[pairs:] = row_masked(body[pairs:], pairs, pairs).astype(BF)
        for p in range(0, pairs, BLOCK):
            n = min(BLOCK, pairs - p)
            y = dot(held[p : p + n].reshape(n * cols, n2), wide[:n2])
            y = y + dot(held[p + 1 : p + 1 + n].reshape(n * cols, n2), wide[n2:])
            y = gathered(y, n, cols, n2)
            for r in range(2):
                lane = pl.ds(r * half, half)
                v = y[:, :, r * half : (r + 1) * half]
                v = v + gain * x_ref[f, p : p + n, r].astype(F32)
                out[i, p : p + n, r] = v[:, 8 : cols - 8].astype(BF)
                side_ref[i, p : p + n, 0:8, lane] = v[:, :8]
                side_ref[i, p : p + n, 8:16, lane] = v[:, cols - 8 :]
                if p == 0:
                    rim_ref[i, 0, :, lane] = v[0, 8 : cols - 8]
                if p + n == pairs:
                    rim_ref[i, 1, :, lane] = v[n - 1, 8 : cols - 8]
        copy = pltpu.make_async_copy(
            out.at[i], o_ref.at[f, :, :, pl.ds(8, cols - 16)], sems.at[i]
        )
        copy.start()
        copies.append(copy)
    for copy in copies:
        copy.wait()


def last_kernel(r_ref, c_ref, m_ref, wide, d_ref, *refs):
    count = (len(refs) - 7) // 2
    sides, rims = refs[:count], refs[count : 2 * count]
    o_ref, held, left, right, rows, sems = refs[-6:]
    frames, rest, _, n2 = r_ref.shape
    pairs, half = rest - 1, n2 // 2
    cols = c_ref.shape[2]
    column, _, tcols = place()
    later = (lax.axis_index("tm") > 0).astype(F32)
    factor = jnp.full((1, n2), 1.0, F32) * later
    ends, rim = [], []
    for f in range(frames):
        factor = factor * twice(d_ref, f)
        far = factor.reshape(1, 1, n2)
        e = r_ref[f] + far * m_ref[: pairs + 1].astype(F32)
        col = lax.broadcasted_iota(jnp.int32, e.shape, 1)
        e = jnp.where(((col == 2) & (column == tcols - 1)) | ((col == 5) & (column == 0)), 0.0, e)
        ends.append(row_masked(e, 0, pairs))
        more = m_ref[pairs + 1 :].astype(F32).reshape(2, cols, n2)
        rim.append(row_masked(c_ref[f] + far * more, 0, 1).astype(BF))
    for f in range(0, frames, 2):
        e = ends[f]
        if f + 1 < frames:
            col = lax.broadcasted_iota(jnp.int32, e.shape, 1)
            own = (col == 1) | (col == 2) | (col == 5) | (col == 6)
            e = jnp.where(own, e, pltpu.roll(ends[f + 1], 2, 1))
        held[f // 2] = e.astype(BF)
    edge_rows = []
    for side in range(2):
        v = jnp.stack([rim[f][side] for f in range(frames)]).reshape(frames * cols, n2)
        y = dot(v, wide[n2:] if side else wide[:n2])
        edge_rows.append(gathered(y, frames, cols, n2))
    copies = []
    for f in range(frames):
        if f % 2 == 0:
            e = held[f // 2]
            y = dot(e[:pairs].reshape(pairs * 8, n2), wide[:n2])
            y = y + dot(e[1:].reshape(pairs * 8, n2), wide[n2:])
            y = y.reshape(pairs, 8, 3 * n2)
            y0, y1, y2 = y[:, :, :n2], y[:, :, n2 : 2 * n2], y[:, :, 2 * n2 :]
        col = lax.broadcasted_iota(jnp.int32, (pairs, 8, n2), 1)
        a, b, d, g = (3, 2, 5, 6) if f % 2 == 0 else (1, 0, 3, 4)
        near = jnp.where(col < 2, pltpu.roll(y0, a, 1), 0.0)
        near = near + jnp.where(col == 0, pltpu.roll(y1, b, 1) if b else y1, 0.0)
        far = jnp.where(col >= 6, pltpu.roll(y2, d, 1), 0.0)
        far = far + jnp.where(col == 7, pltpu.roll(y1, g, 1), 0.0)
        which, i = divmod(f, sides[0].shape[0])
        for at, part, ref, base in ((0, near, left, 0), (8, far, right, cols - 8)):
            total = sides[which][i, :, at : at + 8] + part
            for r in range(2):
                ref[f, :, r] = total[:, :, r * half : (r + 1) * half].astype(BF)
                lane = slice(r * half, (r + 1) * half)
                top = total[:1, :, lane] + edge_rows[0][f : f + 1, base : base + 8, lane]
                low = total[pairs - 1 :, :, lane] + edge_rows[1][f : f + 1, base : base + 8, lane]
                ref[f, 0:1, r] = top.astype(BF)
                ref[f, pairs - 1 :, r] = low.astype(BF)
        for k in range(2):
            v = rims[which][i, k] + edge_rows[k][f, 8 : cols - 8]
            for r in range(2):
                rows[f, k, r] = v[:, r * half : (r + 1) * half].astype(BF)
        ends_of = ((0, 0), (pairs - 1, 1))
        mine = [
            (left.at[f], o_ref.at[f, :, :, pl.ds(0, 8)]),
            (right.at[f], o_ref.at[f, :, :, pl.ds(cols - 8, 8)]),
            *((rows.at[f, k], o_ref.at[f, p, :, pl.ds(8, cols - 16)]) for p, k in ends_of),
        ]
        for k, (source, target) in enumerate(mine):
            copy = pltpu.make_async_copy(source, target, sems.at[f, k])
            copy.start()
            copies.append(copy)
    for copy in copies:
        copy.wait()


def call(body, outs, ins, scratch=(), in_specs=None, out_specs=None, aliases=None):
    return pl.pallas_call(
        body,
        out_shape=outs,
        in_specs=in_specs or [VM] * len(ins),
        out_specs=out_specs if out_specs is not None else jax.tree.map(lambda _: VM, outs),
        scratch_shapes=list(scratch),
        compiler_params=pltpu.CompilerParams(vmem_limit_bytes=LIMIT),
        input_output_aliases=aliases or {},
    )(*ins)


def per_device(frames, w_in, w_out, decay, skip):
    shape = jax.ShapeDtypeStruct
    count, _, rows, cols, c = frames.shape
    n2 = 2 * w_in.shape[3]
    pairs = rows // 2
    video = frames.reshape(count, pairs, 2, cols, c)
    side = shape((count, pairs, 2, 2, c), BF)
    across = shape((count, cols + 8, 2 * c), BF)
    here, side_a, side_b = call(
        pack_kernel,
        (shape(video.shape, BF), side, side),
        (pltpu.with_memory_space_constraint(video, pltpu.HBM),),
        [pltpu.SemaphoreType.DMA((count,))],
        in_specs=[pl.BlockSpec(memory_space=pltpu.HBM)],
    )
    wide_in = shape((4 * c, 3 * n2), BF)
    wide_out = shape((2 * n2, 6 * c), BF)
    head = blocks(pairs)[0]
    pre = call(
        early_kernel,
        shape((count, head[-1][0] + head[-1][1], cols, n2), F32),
        (here, w_in, decay),
        [pltpu.VMEM(wide_in.shape, BF)],
    )
    side_a, side_b, pre = lax.optimization_barrier((side_a, side_b, pre))
    from_a = swapped(side_a, True, 0)
    from_b = swapped(side_b, True, 1)
    local, message, wide_in = call(
        main_kernel,
        (
            shape((count, pairs + 1, cols, n2), F32),
            shape((pairs + 1, cols, n2), BF),
            wide_in,
        ),
        (here, w_in, decay, pre),
    )
    before = onward(message)
    from_a, from_b, local = lax.optimization_barrier((from_a, from_b, local))
    row_a, row_b = call(
        edge_kernel,
        (across, across),
        (here, from_a, from_b),
        [pltpu.VMEM((2 * count, 1, 8, 2 * c), BF)],
    )
    rows_a = swapped(row_a, False, 0)
    rows_b = swapped(row_b, False, 1)
    edge_states = shape((count, pairs + 1, 8, n2), F32)
    partial = call(
        inner_kernel,
        edge_states,
        (here, from_a, from_b, wide_in, decay),
        [pltpu.VMEM((count, pairs, 8, 2 * c), BF)],
    )
    part = count // 2

    def read(first, weight, mixed, local):
        given = (local, before, weight, decay, skip.reshape(1, c), here)
        extra = [] if first == 0 else [mixed]
        outs = (
            shape(video.shape, BF),
            shape((part, pairs, 16, n2), F32),
            shape((part, 2, cols - 16, n2), F32),
        )
        more = (wide_out,) if first == 0 else ()
        return call(
            functools.partial(read_kernel, first),
            (*outs, *more),
            (*given, *extra),
            [
                pltpu.VMEM((pairs + 1, cols, n2), BF),
                pltpu.VMEM((part, pairs, 2, cols - 16, c), BF),
                pltpu.SemaphoreType.DMA((part,)),
            ],
            in_specs=[VM] * len(given) + [ANY] * len(extra),
            out_specs=(ANY, *[VM] * (len(outs) + len(more) - 1)),
            aliases={len(given): 0} if extra else {},
        )

    mixed, side_0, rim_0, wide_out = read(0, w_out, None, local)
    rows_a, rows_b, partial, side_0, local = lax.optimization_barrier(
        (rows_a, rows_b, partial, side_0, local)
    )
    ends, rim, message = call(
        ring_kernel,
        (edge_states, shape((count, 2, cols, n2), F32), shape((pairs + 1 + cols // 4, 8, n2), BF)),
        (rows_a, rows_b, partial, wide_in, decay),
    )
    ring_before = onward(message)
    mixed, side_1, rim_1 = read(part, wide_out, mixed, local)
    ring_before, side_1 = lax.optimization_barrier((ring_before, side_1))
    given = (ends, rim, ring_before, wide_out, decay, side_0, side_1, rim_0, rim_1)
    mixed = call(
        last_kernel,
        shape(video.shape, BF),
        (*given, mixed),
        [
            pltpu.VMEM(((count + 1) // 2, pairs + 1, 8, n2), BF),
            pltpu.VMEM((count, pairs, 2, 8, c), BF),
            pltpu.VMEM((count, pairs, 2, 8, c), BF),
            pltpu.VMEM((count, 2, 2, cols - 16, c), BF),
            pltpu.SemaphoreType.DMA((count, 4)),
        ],
        in_specs=[VM] * len(given) + [ANY],
        out_specs=ANY,
        aliases={len(given): 0},
    )
    return mixed.reshape(count, 1, rows, cols, c)


def solution(mesh):
    return jax.shard_map(
        per_device,
        mesh=mesh,
        in_specs=(P("tm", "tile", None, None, None), P(), P(), P("tm", None), P()),
        out_specs=P("tm", "tile", None, None, None),
        check_vma=False,
    )
```

```python
import functools

import jax
import jax.numpy as jnp
from jax import lax
from jax.experimental import pallas as pl
from jax.experimental.pallas import tpu as pltpu
from jax.sharding import PartitionSpec as P

TROWS = 4
BF = jnp.bfloat16
F32 = jnp.float32
LIMIT = 24 << 20
BLOCK = 16
VM = pl.BlockSpec(memory_space=pltpu.VMEM)
ANY = pl.BlockSpec(memory_space=pl.ANY)


def swapped(value, across, first, spare=False):
    count = lax.axis_size("tile")
    tcols = count // TROWS
    there, left = {}, []
    for number in range(count):
        row, column = divmod(number, tcols)
        at, size = (column, tcols) if across else (row, TROWS)
        other = at + 1 if at >= first and (at - first) % 2 == 0 else at - 1
        me = (number + 1) % count
        if first <= other < size:
            there[me] = ((row * tcols + other if across else other * tcols + column) + 1) % count
        else:
            there[me] = me
            left.append(me)
    left.sort()
    if spare:
        for a, b in zip(left[::2], left[1::2]):
            there[a], there[b] = b, a
    return lax.ppermute(value, "tile", sorted(there.items()))


def onward(value):
    groups = lax.axis_size("tm")
    return lax.ppermute(value, "tm", [(i, (i + 1) % groups) for i in range(groups)])


def place():
    count = lax.axis_size("tile")
    tcols = count // TROWS
    number = lax.rem(lax.axis_index("tile") + count - 1, count)
    return lax.rem(number, tcols), lax.div(number, tcols), tcols


def dot(a, b):
    return jnp.dot(a, b, preferred_element_type=F32)


def spread(w_ref, wide):
    c, n = w_ref.shape[2:]
    zero = jnp.zeros((c, n), BF)
    for tap in range(3):
        for row in range(4):
            for out in range(2):
                at = tap * 2 * n + out * n
                k = row - out
                wide[row * c : (row + 1) * c, at : at + n] = w_ref[k, tap] if 0 <= k <= 2 else zero


def gathered(y, pairs, cols, n2):
    y = y.reshape(pairs, cols, 3 * n2)
    left, mid, right = y[:, :, :n2], y[:, :, n2 : 2 * n2], y[:, :, 2 * n2 :]
    col = lax.broadcasted_iota(jnp.int32, mid.shape, 1)
    left = jnp.where(col > 0, pltpu.roll(left, 1, 1), 0.0)
    right = jnp.where(col < cols - 1, pltpu.roll(right, cols - 1, 1), 0.0)
    return mid + left + right


def gathered_edge(y, pairs, n2):
    y = y.reshape(pairs, 8, 3 * n2)
    left, mid, right = y[:, :, :n2], y[:, :, n2 : 2 * n2], y[:, :, 2 * n2 :]
    col = lax.broadcasted_iota(jnp.int32, mid.shape, 1)
    full = (col == 2) | (col == 5)
    left = jnp.where(full | (col == 6), pltpu.roll(left, 1, 1), 0.0)
    right = jnp.where(full | (col == 1), pltpu.roll(right, 7, 1), 0.0)
    return jnp.where(full, mid, 0.0) + left + right


def blocks(pairs):
    cut = pairs // 4 + 1
    head = [(0, 1), (1, cut - 1)]
    return head, [*((q, min(BLOCK, pairs - q)) for q in range(cut, pairs, BLOCK)), (pairs, 1)]


def ahead():
    return lax.axis_index("tile") == 0


def own_states(x_ref, wide, d_ref, s_ref, m_ref, chosen):
    frames, pairs, _, cols, c = x_ref.shape
    n2 = s_ref.shape[3]

    def rows(f, p, n):
        return jnp.concatenate(
            [x_ref[f, p : p + n, r].reshape(n * cols, c) for r in range(2)], axis=-1
        )

    for q, n in chosen:
        state = None
        for f in range(frames):
            y = None
            if q > 0:
                y = dot(rows(f, q - 1, n), wide[: 2 * c])
            if q < pairs:
                low = dot(rows(f, q, n), wide[2 * c :])
                y = low if y is None else y + low
            y = gathered(y, n, cols, n2)
            state = y if f == 0 else twice(d_ref, f).reshape(1, 1, n2) * state + y
            s_ref[f, q : q + n] = state
        if m_ref is not None:
            m_ref[q : q + n] = state.astype(BF)


def early_kernel(x_ref, w_ref, d_ref, s_ref, wide):
    @pl.when(ahead())
    def _():
        spread(w_ref, wide)
        own_states(x_ref, wide, d_ref, s_ref, None, blocks(x_ref.shape[1])[0])


def main_kernel(x_ref, w_ref, d_ref, p_ref, s_ref, m_ref, wide):
    head, tail = blocks(x_ref.shape[1])
    spread(w_ref, wide)

    @pl.when(jnp.logical_not(ahead()))
    def _():
        own_states(x_ref, wide, d_ref, s_ref, m_ref, head)

    own_states(x_ref, wide, d_ref, s_ref, m_ref, tail)

    @pl.when(ahead())
    def _():
        done = p_ref.shape[1]
        s_ref[:, :done] = p_ref[...]
        m_ref[:done] = p_ref[p_ref.shape[0] - 1].astype(BF)


def pack_kernel(f_ref, x_ref, a_ref, b_ref, sems):
    frames, _, _, cols, _ = x_ref.shape
    column, _, _ = place()
    even = lax.rem(column, 2) == 0
    copies = [
        pltpu.make_async_copy(f_ref.at[f], x_ref.at[f], sems.at[f]) for f in range(frames)
    ]
    for copy in copies:
        copy.start()
    for f, copy in enumerate(copies):
        copy.wait()
        low, high = x_ref[f, :, :, :2], x_ref[f, :, :, cols - 2 :]
        a_ref[f] = jnp.where(even, high, low)
        b_ref[f] = jnp.where(even, low, high)


def group_of(x_ref, fa_ref, fb_ref, f, p, e_ref, at):
    _, _, _, cols, c = x_ref.shape
    column, _, tcols = place()
    even = lax.rem(column, 2) == 0
    for r in range(2):
        lane = pl.ds(r * c, c)
        fa, fb = fa_ref[f, p, r], fb_ref[f, p, r]
        right = jnp.where(column < tcols - 1, jnp.where(even, fa, fb), 0).astype(BF)
        left = jnp.where(column > 0, jnp.where(even, fb, fa), 0).astype(BF)
        e_ref[at, :, 0:2, lane] = x_ref[f, p, r, cols - 2 :]
        e_ref[at, :, 2:4, lane] = right
        e_ref[at, :, 4:6, lane] = left
        e_ref[at, :, 6:8, lane] = x_ref[f, p, r, :2]


def edge_kernel(x_ref, fa_ref, fb_ref, a_ref, b_ref, e_ref):
    frames, pairs, _, cols, c = x_ref.shape
    _, row, _ = place()
    upper = lax.rem(row, 2) == 0
    for f in range(frames):
        for k, p in enumerate((0, pairs - 1)):
            group_of(x_ref, fa_ref, fb_ref, f, slice(p, p + 1), e_ref, 2 * f + k)
        for r in range(2):
            lane = pl.ds(r * c, c)
            top, bottom = x_ref[f, 0, r], x_ref[f, pairs - 1, r]
            a_ref[f, 0:cols, lane] = jnp.where(upper, bottom, top)
            b_ref[f, 0:cols, lane] = jnp.where(upper, top, bottom)
        top, bottom = e_ref[2 * f, 0], e_ref[2 * f + 1, 0]
        a_ref[f, cols:, :] = jnp.where(upper, bottom, top)
        b_ref[f, cols:, :] = jnp.where(upper, top, bottom)


def twice(ref, f):
    return jnp.concatenate([ref[f : f + 1]] * 2, axis=-1)


def inner_kernel(x_ref, fa_ref, fb_ref, wide, d_ref, r_ref, e_ref):
    frames, pairs, _, c2 = e_ref.shape
    n2 = r_ref.shape[3]
    state = None
    blank = jnp.zeros((8, 3 * n2), F32)
    for f in range(frames):
        group_of(x_ref, fa_ref, fb_ref, f, slice(None), e_ref, f)
        e = e_ref[f].reshape(pairs * 8, c2)
        high, low = dot(e, wide[:c2]), dot(e, wide[c2:])
        y = jnp.concatenate([blank, high]) + jnp.concatenate([low, blank])
        y = gathered_edge(y, pairs + 1, n2)
        state = y if f == 0 else twice(d_ref, f).reshape(1, 1, n2) * state + y
        r_ref[f] = state


def ring_kernel(va_ref, vb_ref, p_ref, wide, d_ref, r_ref, c_ref, m_ref):
    frames, size, c2 = va_ref.shape
    pairs, n2 = r_ref.shape[1] - 1, r_ref.shape[3]
    cols = size - 8
    _, row, _ = place()
    upper = lax.rem(row, 2) == 0
    last = frames - 1
    r_ref[...] = p_ref[...]
    for side, there in enumerate((row > 0, row < TROWS - 1)):
        take_a = upper == (side == 1)
        v = jnp.where(there, jnp.where(take_a, va_ref[...], vb_ref[...]), 0).astype(BF)
        y = dot(v.reshape(frames * size, c2), wide[c2:] if side else wide[:c2])
        y = y.reshape(frames, size, 3 * n2)
        mid = gathered(y[:, :cols], frames, cols, n2)
        end = gathered_edge(y[:, cols:], frames, n2)
        y = jnp.concatenate([mid, end], axis=1)
        at = side * pairs
        state = None
        for f in range(frames):
            state = y[f] if f == 0 else twice(d_ref, f) * state + y[f]
            c_ref[f, side] = state[:cols]
            r_ref[f, at] = p_ref[f, at] + state[cols:]
        for k in range(cols // 8):
            m_ref[pairs + 1 + side * (cols // 8) + k] = state[8 * k : 8 * k + 8].astype(BF)
    m_ref[: pairs + 1] = r_ref[last].astype(BF)


def row_masked(value, q, pairs):
    _, row, _ = place()
    _, _, n2 = value.shape
    pair = lax.broadcasted_iota(jnp.int32, value.shape, 0) + q
    lane = lax.broadcasted_iota(jnp.int32, value.shape, 2)
    off = ((pair == 0) & (lane < n2 // 2) & (row == 0)) | (
        (pair == pairs) & (lane >= n2 // 2) & (row == TROWS - 1)
    )
    return jnp.where(off, 0.0, value)


def read_kernel(first, *refs):
    s_ref, m_ref, w_ref, d_ref, skip_ref, x_ref = refs[:6]
    if first == 0:
        wide = refs[-4]
        spread(w_ref, wide)
        o_ref, side_ref, rim_ref = refs[-7:-4]
    else:
        wide = w_ref
        o_ref, side_ref, rim_ref = refs[-6:-3]
    held, out, sems = refs[-3:]
    _, pairs, _, cols, _ = x_ref.shape
    n2 = s_ref.shape[3]
    half = n2 // 2
    later = (lax.axis_index("tm") > 0).astype(F32)
    gain = skip_ref[...].reshape(1, 1, half)
    factor = jnp.full((1, n2), 1.0, F32) * later
    for f in range(first):
        factor = factor * twice(d_ref, f)
    copies = []
    for i in range(side_ref.shape[0]):
        f = first + i
        factor = factor * twice(d_ref, f)
        body = s_ref[f] + factor.reshape(1, 1, n2) * m_ref[...].astype(F32)
        held[...] = body.astype(BF)
        held[0:1] = row_masked(body[0:1], 0, pairs).astype(BF)
        held[pairs:] = row_masked(body[pairs:], pairs, pairs).astype(BF)
        for p in range(0, pairs, BLOCK):
            n = min(BLOCK, pairs - p)
            y = dot(held[p : p + n].reshape(n * cols, n2), wide[:n2])
            y = y + dot(held[p + 1 : p + 1 + n].reshape(n * cols, n2), wide[n2:])
            y = gathered(y, n, cols, n2)
            for r in range(2):
                lane = pl.ds(r * half, half)
                v = y[:, :, r * half : (r + 1) * half]
                v = v + gain * x_ref[f, p : p + n, r].astype(F32)
                out[i, p : p + n, r] = v[:, 8 : cols - 8].astype(BF)
                side_ref[i, p : p + n, 0:8, lane] = v[:, :8]
                side_ref[i, p : p + n, 8:16, lane] = v[:, cols - 8 :]
                if p == 0:
                    rim_ref[i, 0, :, lane] = v[0, 8 : cols - 8]
                if p + n == pairs:
                    rim_ref[i, 1, :, lane] = v[n - 1, 8 : cols - 8]
        copy = pltpu.make_async_copy(
            out.at[i], o_ref.at[f, :, :, pl.ds(8, cols - 16)], sems.at[i]
        )
        copy.start()
        copies.append(copy)
    for copy in copies:
        copy.wait()


def last_kernel(r_ref, c_ref, m_ref, wide, d_ref, *refs):
    count = (len(refs) - 7) // 2
    sides, rims = refs[:count], refs[count : 2 * count]
    o_ref, held, left, right, rows, sems = refs[-6:]
    frames, rest, _, n2 = r_ref.shape
    pairs, half = rest - 1, n2 // 2
    cols = c_ref.shape[2]
    column, _, tcols = place()
    later = (lax.axis_index("tm") > 0).astype(F32)
    factor = jnp.full((1, n2), 1.0, F32) * later
    ends, rim = [], []
    for f in range(frames):
        factor = factor * twice(d_ref, f)
        far = factor.reshape(1, 1, n2)
        e = r_ref[f] + far * m_ref[: pairs + 1].astype(F32)
        col = lax.broadcasted_iota(jnp.int32, e.shape, 1)
        e = jnp.where(((col == 2) & (column == tcols - 1)) | ((col == 5) & (column == 0)), 0.0, e)
        ends.append(row_masked(e, 0, pairs))
        more = m_ref[pairs + 1 :].astype(F32).reshape(2, cols, n2)
        rim.append(row_masked(c_ref[f] + far * more, 0, 1).astype(BF))
    for f in range(0, frames, 2):
        e = ends[f]
        if f + 1 < frames:
            col = lax.broadcasted_iota(jnp.int32, e.shape, 1)
            own = (col == 1) | (col == 2) | (col == 5) | (col == 6)
            e = jnp.where(own, e, pltpu.roll(ends[f + 1], 2, 1))
        held[f // 2] = e.astype(BF)
    edge_rows = []
    for side in range(2):
        v = jnp.stack([rim[f][side] for f in range(frames)]).reshape(frames * cols, n2)
        y = dot(v, wide[n2:] if side else wide[:n2])
        edge_rows.append(gathered(y, frames, cols, n2))
    copies = []
    for f in range(frames):
        if f % 2 == 0:
            e = held[f // 2]
            y = dot(e[:pairs].reshape(pairs * 8, n2), wide[:n2])
            y = y + dot(e[1:].reshape(pairs * 8, n2), wide[n2:])
            y = y.reshape(pairs, 8, 3 * n2)
            y0, y1, y2 = y[:, :, :n2], y[:, :, n2 : 2 * n2], y[:, :, 2 * n2 :]
        col = lax.broadcasted_iota(jnp.int32, (pairs, 8, n2), 1)
        a, b, d, g = (3, 2, 5, 6) if f % 2 == 0 else (1, 0, 3, 4)
        near = jnp.where(col < 2, pltpu.roll(y0, a, 1), 0.0)
        near = near + jnp.where(col == 0, pltpu.roll(y1, b, 1) if b else y1, 0.0)
        far = jnp.where(col >= 6, pltpu.roll(y2, d, 1), 0.0)
        far = far + jnp.where(col == 7, pltpu.roll(y1, g, 1), 0.0)
        which, i = divmod(f, sides[0].shape[0])
        for at, part, ref, base in ((0, near, left, 0), (8, far, right, cols - 8)):
            total = sides[which][i, :, at : at + 8] + part
            for r in range(2):
                ref[f, :, r] = total[:, :, r * half : (r + 1) * half].astype(BF)
                lane = slice(r * half, (r + 1) * half)
                top = total[:1, :, lane] + edge_rows[0][f : f + 1, base : base + 8, lane]
                low = total[pairs - 1 :, :, lane] + edge_rows[1][f : f + 1, base : base + 8, lane]
                ref[f, 0:1, r] = top.astype(BF)
                ref[f, pairs - 1 :, r] = low.astype(BF)
        for k in range(2):
            v = rims[which][i, k] + edge_rows[k][f, 8 : cols - 8]
            for r in range(2):
                rows[f, k, r] = v[:, r * half : (r + 1) * half].astype(BF)
        ends_of = ((0, 0), (pairs - 1, 1))
        mine = [
            (left.at[f], o_ref.at[f, :, :, pl.ds(0, 8)]),
            (right.at[f], o_ref.at[f, :, :, pl.ds(cols - 8, 8)]),
            *((rows.at[f, k], o_ref.at[f, p, :, pl.ds(8, cols - 16)]) for p, k in ends_of),
        ]
        for k, (source, target) in enumerate(mine):
            copy = pltpu.make_async_copy(source, target, sems.at[f, k])
            copy.start()
            copies.append(copy)
    for copy in copies:
        copy.wait()


def call(body, outs, ins, scratch=(), in_specs=None, out_specs=None, aliases=None):
    return pl.pallas_call(
        body,
        out_shape=outs,
        in_specs=in_specs or [VM] * len(ins),
        out_specs=out_specs if out_specs is not None else jax.tree.map(lambda _: VM, outs),
        scratch_shapes=list(scratch),
        compiler_params=pltpu.CompilerParams(vmem_limit_bytes=LIMIT),
        input_output_aliases=aliases or {},
    )(*ins)


def per_device(frames, w_in, w_out, decay, skip):
    shape = jax.ShapeDtypeStruct
    count, _, rows, cols, c = frames.shape
    n2 = 2 * w_in.shape[3]
    pairs = rows // 2
    video = frames.reshape(count, pairs, 2, cols, c)
    side = shape((count, pairs, 2, 2, c), BF)
    across = shape((count, cols + 8, 2 * c), BF)
    here, side_a, side_b = call(
        pack_kernel,
        (shape(video.shape, BF), side, side),
        (pltpu.with_memory_space_constraint(video, pltpu.HBM),),
        [pltpu.SemaphoreType.DMA((count,))],
        in_specs=[pl.BlockSpec(memory_space=pltpu.HBM)],
    )
    wide_in = shape((4 * c, 3 * n2), BF)
    wide_out = shape((2 * n2, 6 * c), BF)
    head = blocks(pairs)[0]
    pre = call(
        early_kernel,
        shape((count, head[-1][0] + head[-1][1], cols, n2), F32),
        (here, w_in, decay),
        [pltpu.VMEM(wide_in.shape, BF)],
    )
    side_a, side_b, pre = lax.optimization_barrier((side_a, side_b, pre))
    from_a = swapped(side_a, True, 0)
    from_b = swapped(side_b, True, 1)
    local, message, wide_in = call(
        main_kernel,
        (
            shape((count, pairs + 1, cols, n2), F32),
            shape((pairs + 1, cols, n2), BF),
            wide_in,
        ),
        (here, w_in, decay, pre),
    )
    before = onward(message)
    from_a, from_b, local = lax.optimization_barrier((from_a, from_b, local))
    row_a, row_b = call(
        edge_kernel,
        (across, across),
        (here, from_a, from_b),
        [pltpu.VMEM((2 * count, 1, 8, 2 * c), BF)],
    )
    rows_a = swapped(row_a, False, 0)
    rows_b = swapped(row_b, False, 1, True)
    edge_states = shape((count, pairs + 1, 8, n2), F32)
    partial = call(
        inner_kernel,
        edge_states,
        (here, from_a, from_b, wide_in, decay),
        [pltpu.VMEM((count, pairs, 8, 2 * c), BF)],
    )
    part = count // 2

    def read(first, weight, mixed, local):
        given = (local, before, weight, decay, skip.reshape(1, c), here)
        extra = [] if first == 0 else [mixed]
        outs = (
            shape(video.shape, BF),
            shape((part, pairs, 16, n2), F32),
            shape((part, 2, cols - 16, n2), F32),
        )
        more = (wide_out,) if first == 0 else ()
        return call(
            functools.partial(read_kernel, first),
            (*outs, *more),
            (*given, *extra),
            [
                pltpu.VMEM((pairs + 1, cols, n2), BF),
                pltpu.VMEM((part, pairs, 2, cols - 16, c), BF),
                pltpu.SemaphoreType.DMA((part,)),
            ],
            in_specs=[VM] * len(given) + [ANY] * len(extra),
            out_specs=(ANY, *[VM] * (len(outs) + len(more) - 1)),
            aliases={len(given): 0} if extra else {},
        )

    mixed, side_0, rim_0, wide_out = read(0, w_out, None, local)
    rows_a, rows_b, partial, side_0, local = lax.optimization_barrier(
        (rows_a, rows_b, partial, side_0, local)
    )
    ends, rim, message = call(
        ring_kernel,
        (edge_states, shape((count, 2, cols, n2), F32), shape((pairs + 1 + cols // 4, 8, n2), BF)),
        (rows_a, rows_b, partial, wide_in, decay),
    )
    ring_before = onward(message)
    mixed, side_1, rim_1 = read(part, wide_out, mixed, local)
    ring_before, side_1 = lax.optimization_barrier((ring_before, side_1))
    given = (ends, rim, ring_before, wide_out, decay, side_0, side_1, rim_0, rim_1)
    mixed = call(
        last_kernel,
        shape(video.shape, BF),
        (*given, mixed),
        [
            pltpu.VMEM(((count + 1) // 2, pairs + 1, 8, n2), BF),
            pltpu.VMEM((count, pairs, 2, 8, c), BF),
            pltpu.VMEM((count, pairs, 2, 8, c), BF),
            pltpu.VMEM((count, 2, 2, cols - 16, c), BF),
            pltpu.SemaphoreType.DMA((count, 4)),
        ],
        in_specs=[VM] * len(given) + [ANY],
        out_specs=ANY,
        aliases={len(given): 0},
    )
    return mixed.reshape(count, 1, rows, cols, c)


def solution(mesh):
    return jax.shard_map(
        per_device,
        mesh=mesh,
        in_specs=(P("tm", "tile", None, None, None), P(), P(), P("tm", None), P()),
        out_specs=P("tm", "tile", None, None, None),
        check_vma=False,
    )
```

```python
import functools

import jax
import jax.numpy as jnp
from jax import lax
from jax.experimental import pallas as pl
from jax.experimental.pallas import tpu as pltpu
from jax.sharding import PartitionSpec as P

TROWS = 4
BF = jnp.bfloat16
F32 = jnp.float32
LIMIT = 24 << 20
BLOCK = 16
WIDE = 12
VM = pl.BlockSpec(memory_space=pltpu.VMEM)
ANY = pl.BlockSpec(memory_space=pl.ANY)


def swapped(value, across, first, spare=False):
    count = lax.axis_size("tile")
    tcols = count // TROWS
    there, left = {}, []
    for number in range(count):
        row, column = divmod(number, tcols)
        at, size = (column, tcols) if across else (row, TROWS)
        other = at + 1 if at >= first and (at - first) % 2 == 0 else at - 1
        me = (number + 1) % count
        if first <= other < size:
            there[me] = ((row * tcols + other if across else other * tcols + column) + 1) % count
        else:
            there[me] = me
            left.append(me)
    left.sort()
    if spare:
        for a, b in zip(left[::2], left[1::2]):
            there[a], there[b] = b, a
    return lax.ppermute(value, "tile", sorted(there.items()))


def onward(value):
    groups = lax.axis_size("tm")
    return lax.ppermute(value, "tm", [(i, (i + 1) % groups) for i in range(groups)])


def place():
    count = lax.axis_size("tile")
    tcols = count // TROWS
    number = lax.rem(lax.axis_index("tile") + count - 1, count)
    return lax.rem(number, tcols), lax.div(number, tcols), tcols


def dot(a, b):
    return jnp.dot(a, b, preferred_element_type=F32)


def spread(w_ref, wide):
    c, n = w_ref.shape[2:]
    zero = jnp.zeros((c, n), BF)
    for tap in range(3):
        for row in range(4):
            for out in range(2):
                at = tap * 2 * n + out * n
                k = row - out
                wide[row * c : (row + 1) * c, at : at + n] = w_ref[k, tap] if 0 <= k <= 2 else zero


def gathered(y, pairs, cols, n2):
    y = y.reshape(pairs, cols, 3 * n2)
    left, mid, right = y[:, :, :n2], y[:, :, n2 : 2 * n2], y[:, :, 2 * n2 :]
    col = lax.broadcasted_iota(jnp.int32, mid.shape, 1)
    left = jnp.where(col > 0, pltpu.roll(left, 1, 1), 0.0)
    right = jnp.where(col < cols - 1, pltpu.roll(right, cols - 1, 1), 0.0)
    return mid + left + right


def gathered_edge(y, pairs, n2):
    y = y.reshape(pairs, 8, 3 * n2)
    left, mid, right = y[:, :, :n2], y[:, :, n2 : 2 * n2], y[:, :, 2 * n2 :]
    col = lax.broadcasted_iota(jnp.int32, mid.shape, 1)
    full = (col == 2) | (col == 5)
    left = jnp.where(full | (col == 6), pltpu.roll(left, 1, 1), 0.0)
    right = jnp.where(full | (col == 1), pltpu.roll(right, 7, 1), 0.0)
    return jnp.where(full, mid, 0.0) + left + right


def blocks(pairs):
    cut = pairs // 4 + 1
    return [(0, cut)], [(q, min(WIDE, pairs + 1 - q)) for q in range(cut, pairs + 1, WIDE)]


def ahead():
    return lax.axis_index("tile") == 0


def own_states(x_ref, wide, d_ref, s_ref, m_ref, chosen):
    frames, pairs, _, cols, c = x_ref.shape
    n2 = s_ref.shape[3]

    def rows(f, p, n):
        return jnp.concatenate(
            [x_ref[f, p : p + n, r].reshape(n * cols, c) for r in range(2)], axis=-1
        )

    for q, n in chosen:
        state = None
        blank = jnp.zeros((cols, 3 * n2), F32)
        for f in range(frames):
            above, below = max(q - 1, 0), min(q + n, pairs)
            high = dot(rows(f, above, q + n - 1 - above), wide[: 2 * c])
            low = dot(rows(f, q, below - q), wide[2 * c :])
            if q == 0:
                high = jnp.concatenate([blank, high])
            if q + n > pairs:
                low = jnp.concatenate([low, blank])
            y = high + low
            y = gathered(y, n, cols, n2)
            state = y if f == 0 else twice(d_ref, f).reshape(1, 1, n2) * state + y
            s_ref[f, q : q + n] = state
        if m_ref is not None:
            m_ref[q : q + n] = state.astype(BF)


def early_kernel(x_ref, w_ref, d_ref, s_ref, wide):
    @pl.when(ahead())
    def _():
        spread(w_ref, wide)
        own_states(x_ref, wide, d_ref, s_ref, None, blocks(x_ref.shape[1])[0])


def main_kernel(x_ref, w_ref, d_ref, p_ref, s_ref, m_ref, wide):
    head, tail = blocks(x_ref.shape[1])
    spread(w_ref, wide)

    @pl.when(jnp.logical_not(ahead()))
    def _():
        own_states(x_ref, wide, d_ref, s_ref, m_ref, head)

    own_states(x_ref, wide, d_ref, s_ref, m_ref, tail)

    @pl.when(ahead())
    def _():
        done = p_ref.shape[1]
        s_ref[:, :done] = p_ref[...]
        m_ref[:done] = p_ref[p_ref.shape[0] - 1].astype(BF)


def pack_kernel(f_ref, x_ref, a_ref, b_ref, sems):
    frames, _, _, cols, _ = x_ref.shape
    column, _, _ = place()
    even = lax.rem(column, 2) == 0
    copies = [
        pltpu.make_async_copy(f_ref.at[f], x_ref.at[f], sems.at[f]) for f in range(frames)
    ]
    for copy in copies:
        copy.start()
    for f, copy in enumerate(copies):
        copy.wait()
        low, high = x_ref[f, :, :, :2], x_ref[f, :, :, cols - 2 :]
        a_ref[f] = jnp.where(even, high, low)
        b_ref[f] = jnp.where(even, low, high)


def group_of(x_ref, fa_ref, fb_ref, f, p, e_ref, at):
    _, _, _, cols, c = x_ref.shape
    column, _, tcols = place()
    even = lax.rem(column, 2) == 0
    for r in range(2):
        lane = pl.ds(r * c, c)
        fa, fb = fa_ref[f, p, r], fb_ref[f, p, r]
        right = jnp.where(column < tcols - 1, jnp.where(even, fa, fb), 0).astype(BF)
        left = jnp.where(column > 0, jnp.where(even, fb, fa), 0).astype(BF)
        e_ref[at, :, 0:2, lane] = x_ref[f, p, r, cols - 2 :]
        e_ref[at, :, 2:4, lane] = right
        e_ref[at, :, 4:6, lane] = left
        e_ref[at, :, 6:8, lane] = x_ref[f, p, r, :2]


def edge_kernel(x_ref, fa_ref, fb_ref, a_ref, b_ref, e_ref):
    frames, pairs, _, cols, c = x_ref.shape
    _, row, _ = place()
    upper = lax.rem(row, 2) == 0
    for f in range(frames):
        for k, p in enumerate((0, pairs - 1)):
            group_of(x_ref, fa_ref, fb_ref, f, slice(p, p + 1), e_ref, 2 * f + k)
        for r in range(2):
            lane = pl.ds(r * c, c)
            top, bottom = x_ref[f, 0, r], x_ref[f, pairs - 1, r]
            a_ref[f, 0:cols, lane] = jnp.where(upper, bottom, top)
            b_ref[f, 0:cols, lane] = jnp.where(upper, top, bottom)
        top, bottom = e_ref[2 * f, 0], e_ref[2 * f + 1, 0]
        a_ref[f, cols:, :] = jnp.where(upper, bottom, top)
        b_ref[f, cols:, :] = jnp.where(upper, top, bottom)


def twice(ref, f):
    return jnp.concatenate([ref[f : f + 1]] * 2, axis=-1)


def inner_kernel(x_ref, fa_ref, fb_ref, wide, d_ref, r_ref, e_ref):
    frames, pairs, _, c2 = e_ref.shape
    n2 = r_ref.shape[3]
    for f in range(frames):
        group_of(x_ref, fa_ref, fb_ref, f, slice(None), e_ref, f)
    e = e_ref[...].reshape(frames * pairs * 8, c2)
    high = dot(e, wide[:c2]).reshape(frames, pairs * 8, 3 * n2)
    low = dot(e, wide[c2:]).reshape(frames, pairs * 8, 3 * n2)
    blank = jnp.zeros((8, 3 * n2), F32)
    state = None
    for f in range(frames):
        y = jnp.concatenate([blank, high[f]]) + jnp.concatenate([low[f], blank])
        y = gathered_edge(y, pairs + 1, n2)
        state = y if f == 0 else twice(d_ref, f).reshape(1, 1, n2) * state + y
        r_ref[f] = state


def ring_kernel(va_ref, vb_ref, p_ref, wide, d_ref, r_ref, c_ref, m_ref):
    frames, size, c2 = va_ref.shape
    pairs, n2 = r_ref.shape[1] - 1, r_ref.shape[3]
    cols = size - 8
    _, row, _ = place()
    upper = lax.rem(row, 2) == 0
    last = frames - 1
    r_ref[...] = p_ref[...]
    for side, there in enumerate((row > 0, row < TROWS - 1)):
        take_a = upper == (side == 1)
        v = jnp.where(there, jnp.where(take_a, va_ref[...], vb_ref[...]), 0).astype(BF)
        y = dot(v.reshape(frames * size, c2), wide[c2:] if side else wide[:c2])
        y = y.reshape(frames, size, 3 * n2)
        mid = gathered(y[:, :cols], frames, cols, n2)
        end = gathered_edge(y[:, cols:], frames, n2)
        y = jnp.concatenate([mid, end], axis=1)
        at = side * pairs
        state = None
        for f in range(frames):
            state = y[f] if f == 0 else twice(d_ref, f) * state + y[f]
            c_ref[f, side] = state[:cols]
            r_ref[f, at] = p_ref[f, at] + state[cols:]
        for k in range(cols // 8):
            m_ref[pairs + 1 + side * (cols // 8) + k] = state[8 * k : 8 * k + 8].astype(BF)
    m_ref[: pairs + 1] = r_ref[last].astype(BF)


def row_masked(value, q, pairs):
    _, row, _ = place()
    _, _, n2 = value.shape
    pair = lax.broadcasted_iota(jnp.int32, value.shape, 0) + q
    lane = lax.broadcasted_iota(jnp.int32, value.shape, 2)
    off = ((pair == 0) & (lane < n2 // 2) & (row == 0)) | (
        (pair == pairs) & (lane >= n2 // 2) & (row == TROWS - 1)
    )
    return jnp.where(off, 0.0, value)


def read_kernel(first, *refs):
    s_ref, m_ref, w_ref, d_ref, skip_ref, x_ref = refs[:6]
    if first == 0:
        wide = refs[-4]
        spread(w_ref, wide)
        o_ref, side_ref, rim_ref = refs[-7:-4]
    else:
        wide = w_ref
        o_ref, side_ref, rim_ref = refs[-6:-3]
    held, out, sems = refs[-3:]
    _, pairs, _, cols, _ = x_ref.shape
    n2 = s_ref.shape[3]
    half = n2 // 2
    later = (lax.axis_index("tm") > 0).astype(F32)
    gain = skip_ref[...].reshape(1, 1, half)
    factor = jnp.full((1, n2), 1.0, F32) * later
    for f in range(first):
        factor = factor * twice(d_ref, f)
    copies = []
    for i in range(side_ref.shape[0]):
        f = first + i
        factor = factor * twice(d_ref, f)
        body = s_ref[f] + factor.reshape(1, 1, n2) * m_ref[...].astype(F32)
        held[...] = body.astype(BF)
        held[0:1] = row_masked(body[0:1], 0, pairs).astype(BF)
        held[pairs:] = row_masked(body[pairs:], pairs, pairs).astype(BF)
        for p in range(0, pairs, BLOCK):
            n = min(BLOCK, pairs - p)
            y = dot(held[p : p + n].reshape(n * cols, n2), wide[:n2])
            y = y + dot(held[p + 1 : p + 1 + n].reshape(n * cols, n2), wide[n2:])
            y = gathered(y, n, cols, n2)
            for r in range(2):
                lane = pl.ds(r * half, half)
                v = y[:, :, r * half : (r + 1) * half]
                v = v + gain * x_ref[f, p : p + n, r].astype(F32)
                out[i, p : p + n, r] = v[:, 8 : cols - 8].astype(BF)
                side_ref[i, p : p + n, 0:8, lane] = v[:, :8]
                side_ref[i, p : p + n, 8:16, lane] = v[:, cols - 8 :]
                if p == 0:
                    rim_ref[i, 0, :, lane] = v[0, 8 : cols - 8]
                if p + n == pairs:
                    rim_ref[i, 1, :, lane] = v[n - 1, 8 : cols - 8]
        copy = pltpu.make_async_copy(
            out.at[i], o_ref.at[f, :, :, pl.ds(8, cols - 16)], sems.at[i]
        )
        copy.start()
        copies.append(copy)
    for copy in copies:
        copy.wait()


def last_kernel(r_ref, c_ref, m_ref, wide, d_ref, *refs):
    count = (len(refs) - 7) // 2
    sides, rims = refs[:count], refs[count : 2 * count]
    o_ref, held, left, right, rows, sems = refs[-6:]
    frames, rest, _, n2 = r_ref.shape
    pairs, half = rest - 1, n2 // 2
    cols = c_ref.shape[2]
    column, _, tcols = place()
    later = (lax.axis_index("tm") > 0).astype(F32)
    factor = jnp.full((1, n2), 1.0, F32) * later
    ends, rim = [], []
    for f in range(frames):
        factor = factor * twice(d_ref, f)
        far = factor.reshape(1, 1, n2)
        e = r_ref[f] + far * m_ref[: pairs + 1].astype(F32)
        col = lax.broadcasted_iota(jnp.int32, e.shape, 1)
        e = jnp.where(((col == 2) & (column == tcols - 1)) | ((col == 5) & (column == 0)), 0.0, e)
        ends.append(row_masked(e, 0, pairs))
        more = m_ref[pairs + 1 :].astype(F32).reshape(2, cols, n2)
        rim.append(row_masked(c_ref[f] + far * more, 0, 1).astype(BF))
    for f in range(0, frames, 2):
        e = ends[f]
        if f + 1 < frames:
            col = lax.broadcasted_iota(jnp.int32, e.shape, 1)
            own = (col == 1) | (col == 2) | (col == 5) | (col == 6)
            e = jnp.where(own, e, pltpu.roll(ends[f + 1], 2, 1))
        held[f // 2] = e.astype(BF)
    edge_rows = []
    for side in range(2):
        v = jnp.stack([rim[f][side] for f in range(frames)]).reshape(frames * cols, n2)
        y = dot(v, wide[n2:] if side else wide[:n2])
        edge_rows.append(gathered(y, frames, cols, n2))
    copies = []
    size = held.shape[0] * pairs * 8
    both = dot(held[:, :pairs].reshape(size, n2), wide[:n2])
    both = both + dot(held[:, 1:].reshape(size, n2), wide[n2:])
    both = both.reshape(held.shape[0], pairs, 8, 3 * n2)
    for f in range(frames):
        if f % 2 == 0:
            y = both[f // 2]
            y0, y1, y2 = y[:, :, :n2], y[:, :, n2 : 2 * n2], y[:, :, 2 * n2 :]
        col = lax.broadcasted_iota(jnp.int32, (pairs, 8, n2), 1)
        a, b, d, g = (3, 2, 5, 6) if f % 2 == 0 else (1, 0, 3, 4)
        near = jnp.where(col < 2, pltpu.roll(y0, a, 1), 0.0)
        near = near + jnp.where(col == 0, pltpu.roll(y1, b, 1) if b else y1, 0.0)
        far = jnp.where(col >= 6, pltpu.roll(y2, d, 1), 0.0)
        far = far + jnp.where(col == 7, pltpu.roll(y1, g, 1), 0.0)
        which, i = divmod(f, sides[0].shape[0])
        for at, part, ref, base in ((0, near, left, 0), (8, far, right, cols - 8)):
            total = sides[which][i, :, at : at + 8] + part
            for r in range(2):
                ref[f, :, r] = total[:, :, r * half : (r + 1) * half].astype(BF)
                lane = slice(r * half, (r + 1) * half)
                top = total[:1, :, lane] + edge_rows[0][f : f + 1, base : base + 8, lane]
                low = total[pairs - 1 :, :, lane] + edge_rows[1][f : f + 1, base : base + 8, lane]
                ref[f, 0:1, r] = top.astype(BF)
                ref[f, pairs - 1 :, r] = low.astype(BF)
        for k in range(2):
            v = rims[which][i, k] + edge_rows[k][f, 8 : cols - 8]
            for r in range(2):
                rows[f, k, r] = v[:, r * half : (r + 1) * half].astype(BF)
        ends_of = ((0, 0), (pairs - 1, 1))
        mine = [
            (left.at[f], o_ref.at[f, :, :, pl.ds(0, 8)]),
            (right.at[f], o_ref.at[f, :, :, pl.ds(cols - 8, 8)]),
            *((rows.at[f, k], o_ref.at[f, p, :, pl.ds(8, cols - 16)]) for p, k in ends_of),
        ]
        for k, (source, target) in enumerate(mine):
            copy = pltpu.make_async_copy(source, target, sems.at[f, k])
            copy.start()
            copies.append(copy)
    for copy in copies:
        copy.wait()


def call(body, outs, ins, scratch=(), in_specs=None, out_specs=None, aliases=None):
    return pl.pallas_call(
        body,
        out_shape=outs,
        in_specs=in_specs or [VM] * len(ins),
        out_specs=out_specs if out_specs is not None else jax.tree.map(lambda _: VM, outs),
        scratch_shapes=list(scratch),
        compiler_params=pltpu.CompilerParams(vmem_limit_bytes=LIMIT),
        input_output_aliases=aliases or {},
    )(*ins)


def per_device(frames, w_in, w_out, decay, skip):
    shape = jax.ShapeDtypeStruct
    count, _, rows, cols, c = frames.shape
    n2 = 2 * w_in.shape[3]
    pairs = rows // 2
    video = frames.reshape(count, pairs, 2, cols, c)
    side = shape((count, pairs, 2, 2, c), BF)
    across = shape((count, cols + 8, 2 * c), BF)
    here, side_a, side_b = call(
        pack_kernel,
        (shape(video.shape, BF), side, side),
        (pltpu.with_memory_space_constraint(video, pltpu.HBM),),
        [pltpu.SemaphoreType.DMA((count,))],
        in_specs=[pl.BlockSpec(memory_space=pltpu.HBM)],
    )
    wide_in = shape((4 * c, 3 * n2), BF)
    wide_out = shape((2 * n2, 6 * c), BF)
    head = blocks(pairs)[0]
    pre = call(
        early_kernel,
        shape((count, head[-1][0] + head[-1][1], cols, n2), F32),
        (here, w_in, decay),
        [pltpu.VMEM(wide_in.shape, BF)],
    )
    side_a, side_b, pre = lax.optimization_barrier((side_a, side_b, pre))
    from_a = swapped(side_a, True, 0)
    from_b = swapped(side_b, True, 1)
    local, message, wide_in = call(
        main_kernel,
        (
            shape((count, pairs + 1, cols, n2), F32),
            shape((pairs + 1, cols, n2), BF),
            wide_in,
        ),
        (here, w_in, decay, pre),
    )
    before = onward(message)
    from_a, from_b, local = lax.optimization_barrier((from_a, from_b, local))
    row_a, row_b = call(
        edge_kernel,
        (across, across),
        (here, from_a, from_b),
        [pltpu.VMEM((2 * count, 1, 8, 2 * c), BF)],
    )
    rows_a = swapped(row_a, False, 0)
    rows_b = swapped(row_b, False, 1, True)
    edge_states = shape((count, pairs + 1, 8, n2), F32)
    partial = call(
        inner_kernel,
        edge_states,
        (here, from_a, from_b, wide_in, decay),
        [pltpu.VMEM((count, pairs, 8, 2 * c), BF)],
    )
    part = count // 2

    def read(first, weight, mixed, local):
        given = (local, before, weight, decay, skip.reshape(1, c), here)
        extra = [] if first == 0 else [mixed]
        outs = (
            shape(video.shape, BF),
            shape((part, pairs, 16, n2), F32),
            shape((part, 2, cols - 16, n2), F32),
        )
        more = (wide_out,) if first == 0 else ()
        return call(
            functools.partial(read_kernel, first),
            (*outs, *more),
            (*given, *extra),
            [
                pltpu.VMEM((pairs + 1, cols, n2), BF),
                pltpu.VMEM((part, pairs, 2, cols - 16, c), BF),
                pltpu.SemaphoreType.DMA((part,)),
            ],
            in_specs=[VM] * len(given) + [ANY] * len(extra),
            out_specs=(ANY, *[VM] * (len(outs) + len(more) - 1)),
            aliases={len(given): 0} if extra else {},
        )

    mixed, side_0, rim_0, wide_out = read(0, w_out, None, local)
    rows_a, rows_b, partial, side_0, local = lax.optimization_barrier(
        (rows_a, rows_b, partial, side_0, local)
    )
    ends, rim, message = call(
        ring_kernel,
        (edge_states, shape((count, 2, cols, n2), F32), shape((pairs + 1 + cols // 4, 8, n2), BF)),
        (rows_a, rows_b, partial, wide_in, decay),
    )
    ring_before = onward(message)
    mixed, side_1, rim_1 = read(part, wide_out, mixed, local)
    ring_before, side_1 = lax.optimization_barrier((ring_before, side_1))
    given = (ends, rim, ring_before, wide_out, decay, side_0, side_1, rim_0, rim_1)
    mixed = call(
        last_kernel,
        shape(video.shape, BF),
        (*given, mixed),
        [
            pltpu.VMEM(((count + 1) // 2, pairs + 1, 8, n2), BF),
            pltpu.VMEM((count, pairs, 2, 8, c), BF),
            pltpu.VMEM((count, pairs, 2, 8, c), BF),
            pltpu.VMEM((count, 2, 2, cols - 16, c), BF),
            pltpu.SemaphoreType.DMA((count, 4)),
        ],
        in_specs=[VM] * len(given) + [ANY],
        out_specs=ANY,
        aliases={len(given): 0},
    )
    return mixed.reshape(count, 1, rows, cols, c)


def solution(mesh):
    return jax.shard_map(
        per_device,
        mesh=mesh,
        in_specs=(P("tm", "tile", None, None, None), P(), P(), P("tm", None), P()),
        out_specs=P("tm", "tile", None, None, None),
        check_vma=False,
    )
```

```python
import functools

import jax
import jax.numpy as jnp
from jax import lax
from jax.experimental import pallas as pl
from jax.experimental.pallas import tpu as pltpu
from jax.sharding import PartitionSpec as P

TROWS = 4
BF = jnp.bfloat16
F32 = jnp.float32
LIMIT = 24 << 20
WIDE = 12
VM = pl.BlockSpec(memory_space=pltpu.VMEM)
ANY = pl.BlockSpec(memory_space=pl.ANY)


def swapped(value, across, first, spare=False):
    count = lax.axis_size("tile")
    tcols = count // TROWS
    there, left = {}, []
    for number in range(count):
        row, column = divmod(number, tcols)
        at, size = (column, tcols) if across else (row, TROWS)
        other = at + 1 if at >= first and (at - first) % 2 == 0 else at - 1
        me = (number + 1) % count
        if first <= other < size:
            there[me] = ((row * tcols + other if across else other * tcols + column) + 1) % count
        else:
            there[me] = me
            left.append(me)
    left.sort()
    if spare:
        for a, b in zip(left[::2], left[1::2]):
            there[a], there[b] = b, a
    return lax.ppermute(value, "tile", sorted(there.items()))


def onward(value):
    groups = lax.axis_size("tm")
    return lax.ppermute(value, "tm", [(i, (i + 1) % groups) for i in range(groups)])


def place():
    count = lax.axis_size("tile")
    tcols = count // TROWS
    number = lax.rem(lax.axis_index("tile") + count - 1, count)
    return lax.rem(number, tcols), lax.div(number, tcols), tcols


def dot(a, b):
    return jnp.dot(a, b, preferred_element_type=F32)


def spread(w_ref, wide):
    c, n = w_ref.shape[2:]
    zero = jnp.zeros((c, n), BF)
    for tap in range(3):
        for row in range(4):
            for out in range(2):
                at = tap * 2 * n + out * n
                k = row - out
                wide[row * c : (row + 1) * c, at : at + n] = w_ref[k, tap] if 0 <= k <= 2 else zero


def gathered(y, pairs, cols, n2):
    y = y.reshape(pairs, cols, 3 * n2)
    left, mid, right = y[:, :, :n2], y[:, :, n2 : 2 * n2], y[:, :, 2 * n2 :]
    col = lax.broadcasted_iota(jnp.int32, mid.shape, 1)
    left = jnp.where(col > 0, pltpu.roll(left, 1, 1), 0.0)
    right = jnp.where(col < cols - 1, pltpu.roll(right, cols - 1, 1), 0.0)
    return mid + left + right


def gathered_edge(y, pairs, n2):
    y = y.reshape(pairs, 8, 3 * n2)
    left, mid, right = y[:, :, :n2], y[:, :, n2 : 2 * n2], y[:, :, 2 * n2 :]
    col = lax.broadcasted_iota(jnp.int32, mid.shape, 1)
    full = (col == 2) | (col == 5)
    left = jnp.where(full | (col == 6), pltpu.roll(left, 1, 1), 0.0)
    right = jnp.where(full | (col == 1), pltpu.roll(right, 7, 1), 0.0)
    return jnp.where(full, mid, 0.0) + left + right


def blocks(pairs):
    cut = pairs // 4 + 1
    return [(0, cut)], [(q, min(WIDE, pairs + 1 - q)) for q in range(cut, pairs + 1, WIDE)]


def ahead():
    return lax.axis_index("tile") == 0


def own_states(x_ref, wide, d_ref, s_ref, m_ref, chosen):
    frames, pairs, _, cols, c = x_ref.shape
    n2 = s_ref.shape[3]

    def rows(f, p, n):
        return jnp.concatenate(
            [x_ref[f, p : p + n, r].reshape(n * cols, c) for r in range(2)], axis=-1
        )

    for q, n in chosen:
        state = None
        blank = jnp.zeros((cols, 3 * n2), F32)
        for f in range(frames):
            above, below = max(q - 1, 0), min(q + n, pairs)
            high = dot(rows(f, above, q + n - 1 - above), wide[: 2 * c])
            low = dot(rows(f, q, below - q), wide[2 * c :])
            if q == 0:
                high = jnp.concatenate([blank, high])
            if q + n > pairs:
                low = jnp.concatenate([low, blank])
            y = high + low
            y = gathered(y, n, cols, n2)
            state = y if f == 0 else twice(d_ref, f).reshape(1, 1, n2) * state + y
            s_ref[f, q : q + n] = state
        if m_ref is not None:
            m_ref[q : q + n] = state.astype(BF)


def early_kernel(x_ref, w_ref, d_ref, s_ref, wide):
    @pl.when(ahead())
    def _():
        spread(w_ref, wide)
        own_states(x_ref, wide, d_ref, s_ref, None, blocks(x_ref.shape[1])[0])


def main_kernel(x_ref, w_ref, d_ref, p_ref, s_ref, m_ref, wide):
    head, tail = blocks(x_ref.shape[1])
    spread(w_ref, wide)

    @pl.when(jnp.logical_not(ahead()))
    def _():
        own_states(x_ref, wide, d_ref, s_ref, m_ref, head)

    own_states(x_ref, wide, d_ref, s_ref, m_ref, tail)

    @pl.when(ahead())
    def _():
        done = p_ref.shape[1]
        s_ref[:, :done] = p_ref[...]
        m_ref[:done] = p_ref[p_ref.shape[0] - 1].astype(BF)


def pack_kernel(f_ref, x_ref, a_ref, b_ref, sems):
    frames, _, _, cols, _ = x_ref.shape
    column, _, _ = place()
    even = lax.rem(column, 2) == 0
    copies = [
        pltpu.make_async_copy(f_ref.at[f], x_ref.at[f], sems.at[f]) for f in range(frames)
    ]
    for copy in copies:
        copy.start()
    for f, copy in enumerate(copies):
        copy.wait()
        low, high = x_ref[f, :, :, :2], x_ref[f, :, :, cols - 2 :]
        a_ref[f] = jnp.where(even, high, low)
        b_ref[f] = jnp.where(even, low, high)


def group_of(x_ref, fa_ref, fb_ref, f, p, e_ref, at):
    _, _, _, cols, c = x_ref.shape
    column, _, tcols = place()
    even = lax.rem(column, 2) == 0
    for r in range(2):
        lane = pl.ds(r * c, c)
        fa, fb = fa_ref[f, p, r], fb_ref[f, p, r]
        right = jnp.where(column < tcols - 1, jnp.where(even, fa, fb), 0).astype(BF)
        left = jnp.where(column > 0, jnp.where(even, fb, fa), 0).astype(BF)
        e_ref[at, :, 0:2, lane] = x_ref[f, p, r, cols - 2 :]
        e_ref[at, :, 2:4, lane] = right
        e_ref[at, :, 4:6, lane] = left
        e_ref[at, :, 6:8, lane] = x_ref[f, p, r, :2]


def edge_kernel(x_ref, fa_ref, fb_ref, a_ref, b_ref, e_ref):
    frames, pairs, _, cols, c = x_ref.shape
    _, row, _ = place()
    upper = lax.rem(row, 2) == 0
    for f in range(frames):
        for k, p in enumerate((0, pairs - 1)):
            group_of(x_ref, fa_ref, fb_ref, f, slice(p, p + 1), e_ref, 2 * f + k)
        for r in range(2):
            lane = pl.ds(r * c, c)
            top, bottom = x_ref[f, 0, r], x_ref[f, pairs - 1, r]
            a_ref[f, 0:cols, lane] = jnp.where(upper, bottom, top)
            b_ref[f, 0:cols, lane] = jnp.where(upper, top, bottom)
        top, bottom = e_ref[2 * f, 0], e_ref[2 * f + 1, 0]
        a_ref[f, cols:, :] = jnp.where(upper, bottom, top)
        b_ref[f, cols:, :] = jnp.where(upper, top, bottom)


def twice(ref, f):
    return jnp.concatenate([ref[f : f + 1]] * 2, axis=-1)


def inner_kernel(x_ref, fa_ref, fb_ref, wide, d_ref, r_ref, e_ref):
    frames, pairs, _, c2 = e_ref.shape
    n2 = r_ref.shape[3]
    for f in range(frames):
        group_of(x_ref, fa_ref, fb_ref, f, slice(None), e_ref, f)
    e = e_ref[...].reshape(frames * pairs * 8, c2)
    high = dot(e, wide[:c2]).reshape(frames, pairs * 8, 3 * n2)
    low = dot(e, wide[c2:]).reshape(frames, pairs * 8, 3 * n2)
    blank = jnp.zeros((8, 3 * n2), F32)
    state = None
    for f in range(frames):
        y = jnp.concatenate([blank, high[f]]) + jnp.concatenate([low[f], blank])
        y = gathered_edge(y, pairs + 1, n2)
        state = y if f == 0 else twice(d_ref, f).reshape(1, 1, n2) * state + y
        r_ref[f] = state


def ring_kernel(va_ref, vb_ref, p_ref, wide, d_ref, r_ref, c_ref, m_ref):
    frames, size, c2 = va_ref.shape
    pairs, n2 = r_ref.shape[1] - 1, r_ref.shape[3]
    cols = size - 8
    _, row, _ = place()
    upper = lax.rem(row, 2) == 0
    last = frames - 1
    r_ref[...] = p_ref[...]
    for side, there in enumerate((row > 0, row < TROWS - 1)):
        take_a = upper == (side == 1)
        v = jnp.where(there, jnp.where(take_a, va_ref[...], vb_ref[...]), 0).astype(BF)
        y = dot(v.reshape(frames * size, c2), wide[c2:] if side else wide[:c2])
        y = y.reshape(frames, size, 3 * n2)
        mid = gathered(y[:, :cols], frames, cols, n2)
        end = gathered_edge(y[:, cols:], frames, n2)
        y = jnp.concatenate([mid, end], axis=1)
        at = side * pairs
        state = None
        for f in range(frames):
            state = y[f] if f == 0 else twice(d_ref, f) * state + y[f]
            c_ref[f, side] = state[:cols]
            r_ref[f, at] = p_ref[f, at] + state[cols:]
        for k in range(cols // 8):
            m_ref[pairs + 1 + side * (cols // 8) + k] = state[8 * k : 8 * k + 8].astype(BF)
    m_ref[: pairs + 1] = r_ref[last].astype(BF)


def row_masked(value, q, pairs):
    _, row, _ = place()
    _, _, n2 = value.shape
    pair = lax.broadcasted_iota(jnp.int32, value.shape, 0) + q
    lane = lax.broadcasted_iota(jnp.int32, value.shape, 2)
    off = ((pair == 0) & (lane < n2 // 2) & (row == 0)) | (
        (pair == pairs) & (lane >= n2 // 2) & (row == TROWS - 1)
    )
    return jnp.where(off, 0.0, value)


def read_kernel(p, n, *refs):
    s_ref, m_ref, w_ref, d_ref, skip_ref, x_ref = refs[:6]
    if p == 0:
        wide = refs[-4]
        spread(w_ref, wide)
        o_ref, side_ref, rim_ref = refs[-7:-4]
    else:
        wide = w_ref
        o_ref, side_ref, rim_ref = refs[-6:-3]
    held, out, sems = refs[-3:]
    frames, pairs, _, cols, _ = x_ref.shape
    n2 = s_ref.shape[3]
    half = n2 // 2
    later = (lax.axis_index("tm") > 0).astype(F32)
    gain = skip_ref[...].reshape(1, 1, half)
    factor = jnp.full((1, n2), 1.0, F32) * later
    copies = []
    for f in range(frames):
        factor = factor * twice(d_ref, f)
        body = s_ref[f, p : p + n + 1]
        body = body + factor.reshape(1, 1, n2) * m_ref[p : p + n + 1].astype(F32)
        held[...] = body.astype(BF)
        if p == 0:
            held[:1] = row_masked(body[:1], 0, pairs).astype(BF)
        else:
            held[n:] = row_masked(body[n:], pairs, pairs).astype(BF)
        y = dot(held[:n].reshape(n * cols, n2), wide[:n2])
        y = y + dot(held[1:].reshape(n * cols, n2), wide[n2:])
        y = gathered(y, n, cols, n2)
        for r in range(2):
            lane = pl.ds(r * half, half)
            v = y[:, :, r * half : (r + 1) * half]
            v = v + gain * x_ref[f, p : p + n, r].astype(F32)
            out[f, :, r] = v[:, 8 : cols - 8].astype(BF)
            side_ref[f, :, 0:8, lane] = v[:, :8]
            side_ref[f, :, 8:16, lane] = v[:, cols - 8 :]
            rim_ref[f, :, lane] = v[0 if p == 0 else n - 1, 8 : cols - 8]
        copy = pltpu.make_async_copy(
            out.at[f], o_ref.at[f, pl.ds(p, n), :, pl.ds(8, cols - 16)], sems.at[f]
        )
        copy.start()
        copies.append(copy)
    for copy in copies:
        copy.wait()


def last_kernel(r_ref, c_ref, m_ref, wide, d_ref, *refs):
    count = (len(refs) - 7) // 2
    sides, rims = refs[:count], refs[count : 2 * count]
    o_ref, held, left, right, rows, sems = refs[-6:]
    frames, rest, _, n2 = r_ref.shape
    pairs, half = rest - 1, n2 // 2
    cols = c_ref.shape[2]
    column, _, tcols = place()
    later = (lax.axis_index("tm") > 0).astype(F32)
    factor = jnp.full((1, n2), 1.0, F32) * later
    ends, rim = [], []
    for f in range(frames):
        factor = factor * twice(d_ref, f)
        far = factor.reshape(1, 1, n2)
        e = r_ref[f] + far * m_ref[: pairs + 1].astype(F32)
        col = lax.broadcasted_iota(jnp.int32, e.shape, 1)
        e = jnp.where(((col == 2) & (column == tcols - 1)) | ((col == 5) & (column == 0)), 0.0, e)
        ends.append(row_masked(e, 0, pairs))
        more = m_ref[pairs + 1 :].astype(F32).reshape(2, cols, n2)
        rim.append(row_masked(c_ref[f] + far * more, 0, 1).astype(BF))
    for f in range(0, frames, 2):
        e = ends[f]
        if f + 1 < frames:
            col = lax.broadcasted_iota(jnp.int32, e.shape, 1)
            own = (col == 1) | (col == 2) | (col == 5) | (col == 6)
            e = jnp.where(own, e, pltpu.roll(ends[f + 1], 2, 1))
        held[f // 2] = e.astype(BF)
    edge_rows = []
    for side in range(2):
        v = jnp.stack([rim[f][side] for f in range(frames)]).reshape(frames * cols, n2)
        y = dot(v, wide[n2:] if side else wide[:n2])
        edge_rows.append(gathered(y, frames, cols, n2))
    copies = []
    size = held.shape[0] * pairs * 8
    both = dot(held[:, :pairs].reshape(size, n2), wide[:n2])
    both = both + dot(held[:, 1:].reshape(size, n2), wide[n2:])
    both = both.reshape(held.shape[0], pairs, 8, 3 * n2)
    for f in range(frames):
        if f % 2 == 0:
            y = both[f // 2]
            y0, y1, y2 = y[:, :, :n2], y[:, :, n2 : 2 * n2], y[:, :, 2 * n2 :]
        col = lax.broadcasted_iota(jnp.int32, (pairs, 8, n2), 1)
        a, b, d, g = (3, 2, 5, 6) if f % 2 == 0 else (1, 0, 3, 4)
        near = jnp.where(col < 2, pltpu.roll(y0, a, 1), 0.0)
        near = near + jnp.where(col == 0, pltpu.roll(y1, b, 1) if b else y1, 0.0)
        far = jnp.where(col >= 6, pltpu.roll(y2, d, 1), 0.0)
        far = far + jnp.where(col == 7, pltpu.roll(y1, g, 1), 0.0)
        for at, part, ref, base in ((0, near, left, 0), (8, far, right, cols - 8)):
            total = jnp.concatenate([own[f, :, at : at + 8] for own in sides]) + part
            for r in range(2):
                ref[f, :, r] = total[:, :, r * half : (r + 1) * half].astype(BF)
                lane = slice(r * half, (r + 1) * half)
                top = total[:1, :, lane] + edge_rows[0][f : f + 1, base : base + 8, lane]
                low = total[pairs - 1 :, :, lane] + edge_rows[1][f : f + 1, base : base + 8, lane]
                ref[f, 0:1, r] = top.astype(BF)
                ref[f, pairs - 1 :, r] = low.astype(BF)
        for k in range(2):
            v = rims[k][f] + edge_rows[k][f, 8 : cols - 8]
            for r in range(2):
                rows[f, k, r] = v[:, r * half : (r + 1) * half].astype(BF)
        ends_of = ((0, 0), (pairs - 1, 1))
        mine = [
            (left.at[f], o_ref.at[f, :, :, pl.ds(0, 8)]),
            (right.at[f], o_ref.at[f, :, :, pl.ds(cols - 8, 8)]),
            *((rows.at[f, k], o_ref.at[f, p, :, pl.ds(8, cols - 16)]) for p, k in ends_of),
        ]
        for k, (source, target) in enumerate(mine):
            copy = pltpu.make_async_copy(source, target, sems.at[f, k])
            copy.start()
            copies.append(copy)
    for copy in copies:
        copy.wait()


def call(body, outs, ins, scratch=(), in_specs=None, out_specs=None, aliases=None):
    return pl.pallas_call(
        body,
        out_shape=outs,
        in_specs=in_specs or [VM] * len(ins),
        out_specs=out_specs if out_specs is not None else jax.tree.map(lambda _: VM, outs),
        scratch_shapes=list(scratch),
        compiler_params=pltpu.CompilerParams(vmem_limit_bytes=LIMIT),
        input_output_aliases=aliases or {},
    )(*ins)


def per_device(frames, w_in, w_out, decay, skip):
    shape = jax.ShapeDtypeStruct
    count, _, rows, cols, c = frames.shape
    n2 = 2 * w_in.shape[3]
    pairs = rows // 2
    video = frames.reshape(count, pairs, 2, cols, c)
    side = shape((count, pairs, 2, 2, c), BF)
    across = shape((count, cols + 8, 2 * c), BF)
    here, side_a, side_b = call(
        pack_kernel,
        (shape(video.shape, BF), side, side),
        (pltpu.with_memory_space_constraint(video, pltpu.HBM),),
        [pltpu.SemaphoreType.DMA((count,))],
        in_specs=[pl.BlockSpec(memory_space=pltpu.HBM)],
    )
    wide_in = shape((4 * c, 3 * n2), BF)
    wide_out = shape((2 * n2, 6 * c), BF)
    head = blocks(pairs)[0]
    pre = call(
        early_kernel,
        shape((count, head[-1][0] + head[-1][1], cols, n2), F32),
        (here, w_in, decay),
        [pltpu.VMEM(wide_in.shape, BF)],
    )
    side_a, side_b, pre = lax.optimization_barrier((side_a, side_b, pre))
    from_a = swapped(side_a, True, 0)
    from_b = swapped(side_b, True, 1)
    local, message, wide_in = call(
        main_kernel,
        (
            shape((count, pairs + 1, cols, n2), F32),
            shape((pairs + 1, cols, n2), BF),
            wide_in,
        ),
        (here, w_in, decay, pre),
    )
    before = onward(message)
    from_a, from_b, local = lax.optimization_barrier((from_a, from_b, local))
    row_a, row_b = call(
        edge_kernel,
        (across, across),
        (here, from_a, from_b),
        [pltpu.VMEM((2 * count, 1, 8, 2 * c), BF)],
    )
    rows_a = swapped(row_a, False, 0)
    rows_b = swapped(row_b, False, 1, True)
    edge_states = shape((count, pairs + 1, 8, n2), F32)
    partial = call(
        inner_kernel,
        edge_states,
        (here, from_a, from_b, wide_in, decay),
        [pltpu.VMEM((count, pairs, 8, 2 * c), BF)],
    )
    most = 5 * pairs // 8

    def read(p, n, weight, mixed, local):
        given = (local, before, weight, decay, skip.reshape(1, c), here)
        extra = [] if p == 0 else [mixed]
        outs = (
            shape(video.shape, BF),
            shape((count, n, 16, n2), F32),
            shape((count, cols - 16, n2), F32),
        )
        more = (wide_out,) if p == 0 else ()
        return call(
            functools.partial(read_kernel, p, n),
            (*outs, *more),
            (*given, *extra),
            [
                pltpu.VMEM((n + 1, cols, n2), BF),
                pltpu.VMEM((count, n, 2, cols - 16, c), BF),
                pltpu.SemaphoreType.DMA((count,)),
            ],
            in_specs=[VM] * len(given) + [ANY] * len(extra),
            out_specs=(ANY, *[VM] * (len(outs) + len(more) - 1)),
            aliases={len(given): 0} if extra else {},
        )

    mixed, side_0, rim_0, wide_out = read(0, most, w_out, None, local)
    rows_a, rows_b, partial, side_0, local = lax.optimization_barrier(
        (rows_a, rows_b, partial, side_0, local)
    )
    ends, rim, message = call(
        ring_kernel,
        (edge_states, shape((count, 2, cols, n2), F32), shape((pairs + 1 + cols // 4, 8, n2), BF)),
        (rows_a, rows_b, partial, wide_in, decay),
    )
    ring_before = onward(message)
    mixed, side_1, rim_1 = read(most, pairs - most, wide_out, mixed, local)
    ring_before, side_1 = lax.optimization_barrier((ring_before, side_1))
    given = (ends, rim, ring_before, wide_out, decay, side_0, side_1, rim_0, rim_1)
    mixed = call(
        last_kernel,
        shape(video.shape, BF),
        (*given, mixed),
        [
            pltpu.VMEM(((count + 1) // 2, pairs + 1, 8, n2), BF),
            pltpu.VMEM((count, pairs, 2, 8, c), BF),
            pltpu.VMEM((count, pairs, 2, 8, c), BF),
            pltpu.VMEM((count, 2, 2, cols - 16, c), BF),
            pltpu.SemaphoreType.DMA((count, 4)),
        ],
        in_specs=[VM] * len(given) + [ANY],
        out_specs=ANY,
        aliases={len(given): 0},
    )
    return mixed.reshape(count, 1, rows, cols, c)


def solution(mesh):
    return jax.shard_map(
        per_device,
        mesh=mesh,
        in_specs=(P("tm", "tile", None, None, None), P(), P(), P("tm", None), P()),
        out_specs=P("tm", "tile", None, None, None),
        check_vma=False,
    )
```

```python
import functools

import jax
import jax.numpy as jnp
from jax import lax
from jax.experimental import pallas as pl
from jax.experimental.pallas import tpu as pltpu
from jax.sharding import PartitionSpec as P

TROWS = 4
BF = jnp.bfloat16
F32 = jnp.float32
LIMIT = 24 << 20
WIDE = 12
VM = pl.BlockSpec(memory_space=pltpu.VMEM)
ANY = pl.BlockSpec(memory_space=pl.ANY)


def swapped(value, across, first, spare=False):
    count = lax.axis_size("tile")
    tcols = count // TROWS
    there, left = {}, []
    for number in range(count):
        row, column = divmod(number, tcols)
        at, size = (column, tcols) if across else (row, TROWS)
        other = at + 1 if at >= first and (at - first) % 2 == 0 else at - 1
        me = (number + 1) % count
        if first <= other < size:
            there[me] = ((row * tcols + other if across else other * tcols + column) + 1) % count
        else:
            there[me] = me
            left.append(me)
    left.sort()
    if spare:
        for a, b in zip(left[::2], left[1::2]):
            there[a], there[b] = b, a
    return lax.ppermute(value, "tile", sorted(there.items()))


def onward(value):
    groups = lax.axis_size("tm")
    return lax.ppermute(value, "tm", [(i, (i + 1) % groups) for i in range(groups)])


def place():
    count = lax.axis_size("tile")
    tcols = count // TROWS
    number = lax.rem(lax.axis_index("tile") + count - 1, count)
    return lax.rem(number, tcols), lax.div(number, tcols), tcols


def dot(a, b):
    return jnp.dot(a, b, preferred_element_type=F32)


def spread(w_ref, wide):
    c, n = w_ref.shape[2:]
    zero = jnp.zeros((c, n), BF)
    for tap in range(3):
        for row in range(4):
            for out in range(2):
                at = tap * 2 * n + out * n
                k = row - out
                wide[row * c : (row + 1) * c, at : at + n] = w_ref[k, tap] if 0 <= k <= 2 else zero


def gathered(y, pairs, cols, n2):
    y = y.reshape(pairs, cols, 3 * n2)
    left, mid, right = y[:, :, :n2], y[:, :, n2 : 2 * n2], y[:, :, 2 * n2 :]
    col = lax.broadcasted_iota(jnp.int32, mid.shape, 1)
    left = jnp.where(col > 0, pltpu.roll(left, 1, 1), 0.0)
    right = jnp.where(col < cols - 1, pltpu.roll(right, cols - 1, 1), 0.0)
    return mid + left + right


def gathered_edge(y, pairs, n2):
    y = y.reshape(pairs, 8, 3 * n2)
    left, mid, right = y[:, :, :n2], y[:, :, n2 : 2 * n2], y[:, :, 2 * n2 :]
    col = lax.broadcasted_iota(jnp.int32, mid.shape, 1)
    full = (col == 2) | (col == 5)
    left = jnp.where(full | (col == 6), pltpu.roll(left, 1, 1), 0.0)
    right = jnp.where(full | (col == 1), pltpu.roll(right, 7, 1), 0.0)
    return jnp.where(full, mid, 0.0) + left + right


def blocks(pairs):
    cut = pairs // 4 + 2
    return [(0, cut)], [(q, min(WIDE, pairs + 1 - q)) for q in range(cut, pairs + 1, WIDE)]


def ahead():
    return lax.axis_index("tile") == 0


def own_states(x_ref, wide, d_ref, s_ref, m_ref, chosen):
    frames, pairs, _, cols, c = x_ref.shape
    n2 = s_ref.shape[3]

    def rows(f, p, n):
        return jnp.concatenate(
            [x_ref[f, p : p + n, r].reshape(n * cols, c) for r in range(2)], axis=-1
        )

    for q, n in chosen:
        state = None
        blank = jnp.zeros((cols, 3 * n2), F32)
        for f in range(frames):
            above, below = max(q - 1, 0), min(q + n, pairs)
            high = dot(rows(f, above, q + n - 1 - above), wide[: 2 * c])
            low = dot(rows(f, q, below - q), wide[2 * c :])
            if q == 0:
                high = jnp.concatenate([blank, high])
            if q + n > pairs:
                low = jnp.concatenate([low, blank])
            y = high + low
            y = gathered(y, n, cols, n2)
            state = y if f == 0 else twice(d_ref, f).reshape(1, 1, n2) * state + y
            s_ref[f, q : q + n] = state
        if m_ref is not None:
            m_ref[q : q + n] = state.astype(BF)


def early_kernel(x_ref, w_ref, d_ref, s_ref, wide):
    @pl.when(ahead())
    def _():
        spread(w_ref, wide)
        own_states(x_ref, wide, d_ref, s_ref, None, blocks(x_ref.shape[1])[0])


def main_kernel(x_ref, w_ref, d_ref, p_ref, s_ref, m_ref, wide):
    head, tail = blocks(x_ref.shape[1])
    spread(w_ref, wide)

    @pl.when(jnp.logical_not(ahead()))
    def _():
        own_states(x_ref, wide, d_ref, s_ref, m_ref, head)

    own_states(x_ref, wide, d_ref, s_ref, m_ref, tail)

    @pl.when(ahead())
    def _():
        done = p_ref.shape[1]
        s_ref[:, :done] = p_ref[...]
        m_ref[:done] = p_ref[p_ref.shape[0] - 1].astype(BF)


def pack_kernel(f_ref, x_ref, a_ref, b_ref, sems):
    frames, _, _, cols, _ = x_ref.shape
    column, _, _ = place()
    even = lax.rem(column, 2) == 0
    copies = [
        pltpu.make_async_copy(f_ref.at[f], x_ref.at[f], sems.at[f]) for f in range(frames)
    ]
    for copy in copies:
        copy.start()
    for f, copy in enumerate(copies):
        copy.wait()
        low, high = x_ref[f, :, :, :2], x_ref[f, :, :, cols - 2 :]
        a_ref[f] = jnp.where(even, high, low)
        b_ref[f] = jnp.where(even, low, high)


def group_of(x_ref, fa_ref, fb_ref, f, p, e_ref, at):
    _, _, _, cols, c = x_ref.shape
    column, _, tcols = place()
    even = lax.rem(column, 2) == 0
    for r in range(2):
        lane = pl.ds(r * c, c)
        fa, fb = fa_ref[f, p, r], fb_ref[f, p, r]
        right = jnp.where(column < tcols - 1, jnp.where(even, fa, fb), 0).astype(BF)
        left = jnp.where(column > 0, jnp.where(even, fb, fa), 0).astype(BF)
        e_ref[at, :, 0:2, lane] = x_ref[f, p, r, cols - 2 :]
        e_ref[at, :, 2:4, lane] = right
        e_ref[at, :, 4:6, lane] = left
        e_ref[at, :, 6:8, lane] = x_ref[f, p, r, :2]


def edge_kernel(x_ref, fa_ref, fb_ref, a_ref, b_ref, e_ref):
    frames, pairs, _, cols, c = x_ref.shape
    _, row, _ = place()
    upper = lax.rem(row, 2) == 0
    for f in range(frames):
        for k, p in enumerate((0, pairs - 1)):
            group_of(x_ref, fa_ref, fb_ref, f, slice(p, p + 1), e_ref, 2 * f + k)
        for r in range(2):
            lane = pl.ds(r * c, c)
            top, bottom = x_ref[f, 0, r], x_ref[f, pairs - 1, r]
            a_ref[f, 0:cols, lane] = jnp.where(upper, bottom, top)
            b_ref[f, 0:cols, lane] = jnp.where(upper, top, bottom)
        top, bottom = e_ref[2 * f, 0], e_ref[2 * f + 1, 0]
        a_ref[f, cols:, :] = jnp.where(upper, bottom, top)
        b_ref[f, cols:, :] = jnp.where(upper, top, bottom)


def twice(ref, f):
    return jnp.concatenate([ref[f : f + 1]] * 2, axis=-1)


def inner_kernel(x_ref, fa_ref, fb_ref, wide, d_ref, r_ref, e_ref):
    frames, pairs, _, c2 = e_ref.shape
    n2 = r_ref.shape[3]
    for f in range(frames):
        group_of(x_ref, fa_ref, fb_ref, f, slice(None), e_ref, f)
    e = e_ref[...].reshape(frames * pairs * 8, c2)
    high = dot(e, wide[:c2]).reshape(frames, pairs * 8, 3 * n2)
    low = dot(e, wide[c2:]).reshape(frames, pairs * 8, 3 * n2)
    blank = jnp.zeros((8, 3 * n2), F32)
    state = None
    for f in range(frames):
        y = jnp.concatenate([blank, high[f]]) + jnp.concatenate([low[f], blank])
        y = gathered_edge(y, pairs + 1, n2)
        state = y if f == 0 else twice(d_ref, f).reshape(1, 1, n2) * state + y
        r_ref[f] = state


def ring_kernel(va_ref, vb_ref, p_ref, wide, d_ref, r_ref, c_ref, m_ref):
    frames, size, c2 = va_ref.shape
    pairs, n2 = r_ref.shape[1] - 1, r_ref.shape[3]
    cols = size - 8
    _, row, _ = place()
    upper = lax.rem(row, 2) == 0
    last = frames - 1
    r_ref[...] = p_ref[...]
    for side, there in enumerate((row > 0, row < TROWS - 1)):
        take_a = upper == (side == 1)
        v = jnp.where(there, jnp.where(take_a, va_ref[...], vb_ref[...]), 0).astype(BF)
        y = dot(v.reshape(frames * size, c2), wide[c2:] if side else wide[:c2])
        y = y.reshape(frames, size, 3 * n2)
        mid = gathered(y[:, :cols], frames, cols, n2)
        end = gathered_edge(y[:, cols:], frames, n2)
        y = jnp.concatenate([mid, end], axis=1)
        at = side * pairs
        state = None
        for f in range(frames):
            state = y[f] if f == 0 else twice(d_ref, f) * state + y[f]
            c_ref[f, side] = state[:cols]
            r_ref[f, at] = p_ref[f, at] + state[cols:]
        for k in range(cols // 8):
            m_ref[pairs + 1 + side * (cols // 8) + k] = state[8 * k : 8 * k + 8].astype(BF)
    m_ref[: pairs + 1] = r_ref[last].astype(BF)


def row_masked(value, q, pairs):
    _, row, _ = place()
    _, _, n2 = value.shape
    pair = lax.broadcasted_iota(jnp.int32, value.shape, 0) + q
    lane = lax.broadcasted_iota(jnp.int32, value.shape, 2)
    off = ((pair == 0) & (lane < n2 // 2) & (row == 0)) | (
        (pair == pairs) & (lane >= n2 // 2) & (row == TROWS - 1)
    )
    return jnp.where(off, 0.0, value)


def middle_copies(out, o_ref, p, n, sem):
    frames, _, _, width, _ = out.shape
    return [
        pltpu.make_async_copy(
            out.at[f, pl.ds(0, n)], o_ref.at[f, pl.ds(p, n), :, pl.ds(8, width)], sem.at[f]
        )
        for f in range(frames)
    ]


def read_kernel(p, n, *refs):
    s_ref, m_ref, w_ref, d_ref, skip_ref, x_ref = refs[:6]
    frames, pairs, _, cols, _ = x_ref.shape
    copies = []
    if p == 0:
        out, side_ref, rim_ref, wide, held = refs[6:]
        spread(w_ref, wide)
    else:
        wide = w_ref
        before_ref, o_ref, out, side_ref, rim_ref, held, sems = refs[6:]
        copies = middle_copies(before_ref, o_ref, 0, p, sems.at[0])
    for copy in copies:
        copy.start()
    n2 = s_ref.shape[3]
    half = n2 // 2
    later = (lax.axis_index("tm") > 0).astype(F32)
    gain = skip_ref[...].reshape(1, 1, half)
    factor = jnp.full((1, n2), 1.0, F32) * later
    for f in range(frames):
        factor = factor * twice(d_ref, f)
        body = s_ref[f, p : p + n + 1]
        body = body + factor.reshape(1, 1, n2) * m_ref[p : p + n + 1].astype(F32)
        held[...] = body.astype(BF)
        if p == 0:
            held[:1] = row_masked(body[:1], 0, pairs).astype(BF)
        else:
            held[n:] = row_masked(body[n:], pairs, pairs).astype(BF)
        y = dot(held[:n].reshape(n * cols, n2), wide[:n2])
        y = y + dot(held[1:].reshape(n * cols, n2), wide[n2:])
        y = gathered(y, n, cols, n2)
        for r in range(2):
            lane = pl.ds(r * half, half)
            v = y[:, :, r * half : (r + 1) * half]
            v = v + gain * x_ref[f, p : p + n, r].astype(F32)
            out[f, :, r] = v[:, 8 : cols - 8].astype(BF)
            side_ref[f, :, 0:8, lane] = v[:, :8]
            side_ref[f, :, 8:16, lane] = v[:, cols - 8 :]
            rim_ref[f, :, lane] = v[0 if p == 0 else n - 1, 8 : cols - 8]
    for copy in copies:
        copy.wait()


def last_kernel(r_ref, c_ref, m_ref, wide, d_ref, *refs):
    count = (len(refs) - 9) // 2
    sides, rims = refs[:count], refs[count : 2 * count]
    out, _, o_ref, held, left, right, rows, sems, more_sems = refs[-9:]
    frames, rest, _, n2 = r_ref.shape
    pairs, half = rest - 1, n2 // 2
    cols = c_ref.shape[2]
    column, _, tcols = place()
    later = (lax.axis_index("tm") > 0).astype(F32)
    factor = jnp.full((1, n2), 1.0, F32) * later
    ends, rim = [], []
    n = out.shape[1]
    copies = middle_copies(out, o_ref, pairs - n, n - 1, more_sems)
    for copy in copies:
        copy.start()
    for f in range(frames):
        factor = factor * twice(d_ref, f)
        far = factor.reshape(1, 1, n2)
        e = r_ref[f] + far * m_ref[: pairs + 1].astype(F32)
        col = lax.broadcasted_iota(jnp.int32, e.shape, 1)
        e = jnp.where(((col == 2) & (column == tcols - 1)) | ((col == 5) & (column == 0)), 0.0, e)
        ends.append(
            jnp.concatenate(
                [row_masked(e[:1], 0, pairs), e[1:pairs], row_masked(e[pairs:], pairs, pairs)]
            )
        )
        more = m_ref[pairs + 1 :].astype(F32).reshape(2, cols, n2)
        rim.append(row_masked(c_ref[f] + far * more, 0, 1).astype(BF))
    for f in range(0, frames, 2):
        e = ends[f]
        if f + 1 < frames:
            col = lax.broadcasted_iota(jnp.int32, e.shape, 1)
            own = (col == 1) | (col == 2) | (col == 5) | (col == 6)
            e = jnp.where(own, e, pltpu.roll(ends[f + 1], 2, 1))
        held[f // 2] = e.astype(BF)
    edge_rows = []
    for side in range(2):
        v = jnp.stack([rim[f][side] for f in range(frames)]).reshape(frames * cols, n2)
        y = dot(v, wide[n2:] if side else wide[:n2])
        edge_rows.append(gathered(y, frames, cols, n2))
    size = held.shape[0] * pairs * 8
    both = dot(held[:, :pairs].reshape(size, n2), wide[:n2])
    both = both + dot(held[:, 1:].reshape(size, n2), wide[n2:])
    both = both.reshape(held.shape[0], pairs, 8, 3 * n2)
    for f in range(frames):
        if f % 2 == 0:
            y = both[f // 2]
            y0, y1, y2 = y[:, :, :n2], y[:, :, n2 : 2 * n2], y[:, :, 2 * n2 :]
        col = lax.broadcasted_iota(jnp.int32, (pairs, 8, n2), 1)
        a, b, d, g = (3, 2, 5, 6) if f % 2 == 0 else (1, 0, 3, 4)
        near = jnp.where(col < 2, pltpu.roll(y0, a, 1), 0.0)
        near = near + jnp.where(col == 0, pltpu.roll(y1, b, 1) if b else y1, 0.0)
        far = jnp.where(col >= 6, pltpu.roll(y2, d, 1), 0.0)
        far = far + jnp.where(col == 7, pltpu.roll(y1, g, 1), 0.0)
        for at, part, ref, base in ((0, near, left, 0), (8, far, right, cols - 8)):
            total = jnp.concatenate([own[f, :, at : at + 8] for own in sides]) + part
            for r in range(2):
                ref[f, :, r] = total[:, :, r * half : (r + 1) * half].astype(BF)
                lane = slice(r * half, (r + 1) * half)
                top = total[:1, :, lane] + edge_rows[0][f : f + 1, base : base + 8, lane]
                low = total[pairs - 1 :, :, lane] + edge_rows[1][f : f + 1, base : base + 8, lane]
                ref[f, 0:1, r] = top.astype(BF)
                ref[f, pairs - 1 :, r] = low.astype(BF)
        for k in range(2):
            v = rims[k][f] + edge_rows[k][f, 8 : cols - 8]
            for r in range(2):
                rows[f, k, r] = v[:, r * half : (r + 1) * half].astype(BF)
        ends_of = ((0, 0), (pairs - 1, 1))
        mine = [
            (left.at[f], o_ref.at[f, :, :, pl.ds(0, 8)]),
            (right.at[f], o_ref.at[f, :, :, pl.ds(cols - 8, 8)]),
            *((rows.at[f, k], o_ref.at[f, p, :, pl.ds(8, cols - 16)]) for p, k in ends_of),
        ]
        for k, (source, target) in enumerate(mine):
            copy = pltpu.make_async_copy(source, target, sems.at[f, k])
            copy.start()
            copies.append(copy)
    for copy in copies:
        copy.wait()


def call(body, outs, ins, scratch=(), in_specs=None, out_specs=None, aliases=None):
    return pl.pallas_call(
        body,
        out_shape=outs,
        in_specs=in_specs or [VM] * len(ins),
        out_specs=out_specs if out_specs is not None else jax.tree.map(lambda _: VM, outs),
        scratch_shapes=list(scratch),
        compiler_params=pltpu.CompilerParams(vmem_limit_bytes=LIMIT),
        input_output_aliases=aliases or {},
    )(*ins)


def per_device(frames, w_in, w_out, decay, skip):
    shape = jax.ShapeDtypeStruct
    count, _, rows, cols, c = frames.shape
    n2 = 2 * w_in.shape[3]
    pairs = rows // 2
    video = frames.reshape(count, pairs, 2, cols, c)
    side = shape((count, pairs, 2, 2, c), BF)
    across = shape((count, cols + 8, 2 * c), BF)
    here, side_a, side_b = call(
        pack_kernel,
        (shape(video.shape, BF), side, side),
        (pltpu.with_memory_space_constraint(video, pltpu.HBM),),
        [pltpu.SemaphoreType.DMA((count,))],
        in_specs=[pl.BlockSpec(memory_space=pltpu.HBM)],
    )
    wide_in = shape((4 * c, 3 * n2), BF)
    wide_out = shape((2 * n2, 6 * c), BF)
    head = blocks(pairs)[0]
    pre = call(
        early_kernel,
        shape((count, head[-1][0] + head[-1][1], cols, n2), F32),
        (here, w_in, decay),
        [pltpu.VMEM(wide_in.shape, BF)],
    )
    side_a, side_b, pre = lax.optimization_barrier((side_a, side_b, pre))
    from_a = swapped(side_a, True, 0)
    from_b = swapped(side_b, True, 1)
    local, message, wide_in = call(
        main_kernel,
        (
            shape((count, pairs + 1, cols, n2), F32),
            shape((pairs + 1, cols, n2), BF),
            wide_in,
        ),
        (here, w_in, decay, pre),
    )
    before = onward(message)
    from_a, from_b, local = lax.optimization_barrier((from_a, from_b, local))
    row_a, row_b = call(
        edge_kernel,
        (across, across),
        (here, from_a, from_b),
        [pltpu.VMEM((2 * count, 1, 8, 2 * c), BF)],
    )
    rows_a = swapped(row_a, False, 0)
    rows_b = swapped(row_b, False, 1, True)
    edge_states = shape((count, pairs + 1, 8, n2), F32)
    partial = call(
        inner_kernel,
        edge_states,
        (here, from_a, from_b, wide_in, decay),
        [pltpu.VMEM((count, pairs, 8, 2 * c), BF)],
    )
    most = 3 * pairs // 4

    def read(p, n, weight, out, local):
        given = (local, before, weight, decay, skip.reshape(1, c), here)
        outs = (
            shape((count, n, 2, cols - 16, c), BF),
            shape((count, n, 16, n2), F32),
            shape((count, cols - 16, n2), F32),
        )
        first = p == 0
        sems = [] if first else [pltpu.SemaphoreType.DMA((1, count))]
        return call(
            functools.partial(read_kernel, p, n),
            (*outs, wide_out) if first else (shape(video.shape, BF), *outs),
            given if first else (*given, out),
            [pltpu.VMEM((n + 1, cols, n2), BF), *sems],
            out_specs=(VM if first else ANY, VM, VM, VM),
        )

    out_0, side_0, rim_0, wide_out = read(0, most, w_out, None, local)
    rows_a, rows_b, partial, side_0, local = lax.optimization_barrier(
        (rows_a, rows_b, partial, side_0, local)
    )
    ends, rim, message = call(
        ring_kernel,
        (edge_states, shape((count, 2, cols, n2), F32), shape((pairs + 1 + cols // 4, 8, n2), BF)),
        (rows_a, rows_b, partial, wide_in, decay),
    )
    ring_before = onward(message)
    mixed, out_1, side_1, rim_1 = read(most, pairs - most, wide_out, out_0, local)
    ring_before, side_1 = lax.optimization_barrier((ring_before, side_1))
    given = (ends, rim, ring_before, wide_out, decay, side_0, side_1, rim_0, rim_1, out_1)
    mixed = call(
        last_kernel,
        shape(video.shape, BF),
        (*given, mixed),
        [
            pltpu.VMEM(((count + 1) // 2, pairs + 1, 8, n2), BF),
            pltpu.VMEM((count, pairs, 2, 8, c), BF),
            pltpu.VMEM((count, pairs, 2, 8, c), BF),
            pltpu.VMEM((count, 2, 2, cols - 16, c), BF),
            pltpu.SemaphoreType.DMA((count, 4)),
            pltpu.SemaphoreType.DMA((count,)),
        ],
        in_specs=[VM] * len(given) + [ANY],
        out_specs=ANY,
        aliases={len(given): 0},
    )
    return mixed.reshape(count, 1, rows, cols, c)


def solution(mesh):
    return jax.shard_map(
        per_device,
        mesh=mesh,
        in_specs=(P("tm", "tile", None, None, None), P(), P(), P("tm", None), P()),
        out_specs=P("tm", "tile", None, None, None),
        check_vma=False,
    )
```
